32 devices in a mesh: mesh: 8 (over y, x, core), state: 4 (over z).
Axes of the slice: x: 2, y: 2, z: 4, core: 2. Of those that a mesh axis runs over, the one named last changes fastest.
Arguments:
- kern_blocks: bfloat16 [192, 16, 128, 128], P('mesh'), may hold values from 4.296875e-06 to 0.13744531
- kern_cols: int32 [192, 16], P('mesh'), may hold values from 0 to 191, as said below
- state_kernel: bfloat16 [512, 512], replicated, may hold values from 0 to 0.61, as said below
- start_v: float32 [24576, 512], P('mesh', 'state'), may hold values from 0.5 to 5
- mu: float32 [24576, 512], P(('mesh', 'state')), may hold values from 0.2 to 2
- nu: float32 [24576, 512], P('mesh', 'state'), may hold values from 0.2 to 2
Outputs:
- potential_u: float32 [24576, 512], P(('mesh', 'state'))
- potential_v: float32 [24576, 512], P('mesh', 'state')
The draws below stay inside these ranges and needn't reach their ends.
Inputs may be any that keep to these rules, and one draw needn't show every extreme that they name: `kern_cols`: each block row names 16 different block columns, its own block among them. The block rows held by index d of mesh (rows d * 24 to (d + 1) * 24 - 1) refer, among the blocks of index d - 1 and d + 1 (wrapping around 8), only to the last 6 blocks of d - 1 and the first 6 blocks of d + 1, and to all of them; among the blocks of every other index, to at most 2 distinct blocks, and to exactly 2 of index d + 2. How many other indices they reach differs from index to index. `state_kernel`: each row has a positive diagonal entry.
All inputs are finite; a program needn't handle non-finite values.
Results may differ from the reference program's by a relative error of at most 0.0033.
Values may be sent and summed in bfloat16 or wider, within the bound.
No kernel may reach another device: no remote copies, remote signals or barrier semaphores. Data moves between devices by JAX's collectives and lax.ppermute only.
A program may use at most 192 MiB of HBM per device.

```python
import math
import jax
import jax.numpy as jnp
from jax import lax

B = 128
DEG = 16
N2 = 512
NBR_DEV = 24
CAP_FAR = 2
ITERS = 2
CAP_NEAR = 6
NB = 192
N1 = 24576
N_MESH = 8


def draw_kern_blocks(key, part):
    key_back = jax.random.fold_in(key, 21)
    key_peak = jax.random.fold_in(key, 22)
    key_gain = jax.random.fold_in(key, 23)
    key_shift = jax.random.fold_in(key, 24)
    row_ids = jnp.arange(B, dtype=jnp.int32)[:, None]
    col_ids = jnp.arange(B, dtype=jnp.int32)[None, :]
    offset = jax.random.randint(key_shift, (NB, DEG, 1, 1), 0, B, dtype=jnp.int32)
    on_peak = col_ids[None, None] == (row_ids[None, None] + offset) % B
    back_draw = jax.random.uniform(key_back, (NB, DEG, B, B), jnp.float32)
    peak_draw = jax.random.uniform(key_peak, (NB, DEG, B, 1), jnp.float32)
    gain_draw = jax.random.uniform(key_gain, (NB, DEG, 1, 1), jnp.float32)
    background = 0.2 * jnp.exp(back_draw * math.log(8.0)) / B
    peak_value = jnp.exp(peak_draw * math.log(3.0))
    gain_value = 0.045 * jnp.exp(gain_draw * math.log(16.0)) / DEG
    entries = gain_value * (background + jnp.where(on_peak, peak_value, 0.0))
    return entries.astype(jnp.bfloat16)


def draw_state_kernel(key, part):
    key_order = jax.random.fold_in(key, 31)
    key_factor = jax.random.fold_in(key, 32)
    position = jax.random.permutation(key_order, N2).astype(jnp.int32)
    spacing = jnp.abs(position[:, None] - position[None, :])
    cycle_gap = jnp.minimum(spacing, N2 - spacing).astype(jnp.float32)
    profile = jnp.exp(-cycle_gap * cycle_gap / 4.0)
    factor_draw = jax.random.uniform(key_factor, (N2, N2), jnp.float32)
    factor = 0.25 * jnp.exp(factor_draw * math.log(16.0))
    return (0.15 * factor * profile).astype(jnp.bfloat16)


def draw_kern_cols(key, part):
    peer_count = NB // NBR_DEV
    far_count = peer_count - 3
    pool_size = NBR_DEV + 2 * CAP_NEAR + far_count * CAP_FAR
    devices = jnp.arange(peer_count, dtype=jnp.int32)
    local_ids = devices[:, None] * NBR_DEV + jnp.arange(NBR_DEV, dtype=jnp.int32)[None, :]
    left_ids = ((devices + peer_count - 1) % peer_count)[:, None] * NBR_DEV + (NBR_DEV - CAP_NEAR + jnp.arange(CAP_NEAR, dtype=jnp.int32))[None, :]
    right_ids = ((devices + 1) % peer_count)[:, None] * NBR_DEV + jnp.arange(CAP_NEAR, dtype=jnp.int32)[None, :]
    far_peer = (devices[:, None] + 2 + jnp.arange(far_count, dtype=jnp.int32)[None, :]) % peer_count
    key_first = jax.random.fold_in(key, 11)
    key_step = jax.random.fold_in(key, 12)
    key_count = jax.random.fold_in(key, 13)
    key_score = jax.random.fold_in(key, 14)
    first = jax.random.randint(key_first, (peer_count, far_count), 0, NBR_DEV, dtype=jnp.int32)
    stride = jax.random.randint(key_step, (peer_count, far_count), 1, NBR_DEV, dtype=jnp.int32)
    far_local = (first[:, :, None] + jnp.arange(CAP_FAR, dtype=jnp.int32)[None, None, :] * stride[:, :, None]) % NBR_DEV
    far_ids = (far_peer[:, :, None] * NBR_DEV + far_local).reshape(peer_count, far_count * CAP_FAR)
    candidates = jnp.concatenate([local_ids, left_ids, right_ids, far_ids], axis=1)
    in_use = jax.random.randint(key_count, (peer_count,), 1, far_count + 1, dtype=jnp.int32)
    extra_count = 2 * CAP_NEAR + far_count * CAP_FAR
    extra_pos = jnp.arange(extra_count, dtype=jnp.int32)
    far_order = jnp.maximum(extra_pos - 2 * CAP_NEAR, 0) // CAP_FAR
    extra_active = (extra_pos < 2 * CAP_NEAR)[None, :] | (far_order[None, :] < in_use[:, None])
    extra_row = extra_pos % NBR_DEV
    row_ids = jnp.arange(NBR_DEV, dtype=jnp.int32)
    local_forced = (row_ids[:, None] == row_ids[None, :]).astype(jnp.int32)
    extra_forced = (row_ids[None, :, None] == extra_row[None, None, :]) & extra_active[:, None, :]
    forced = jnp.concatenate([jnp.broadcast_to(local_forced[None], (peer_count, NBR_DEV, NBR_DEV)), extra_forced.astype(jnp.int32)], axis=2)
    active = jnp.concatenate([jnp.ones((peer_count, NBR_DEV), jnp.int32), extra_active.astype(jnp.int32)], axis=1)
    level = jnp.where(forced > 0, 3, jnp.broadcast_to(active[:, None, :], forced.shape))
    noise = jax.random.randint(key_score, (peer_count, NBR_DEV, pool_size), 0, 4096, dtype=jnp.int32)
    scores = level * 1048576 + noise * pool_size + jnp.arange(pool_size, dtype=jnp.int32)[None, None, :]
    _, picked = lax.top_k(scores, DEG)
    chosen = jnp.take_along_axis(jnp.broadcast_to(candidates[:, None, :], scores.shape), picked, axis=2)
    return chosen.reshape(NB, DEG).astype(jnp.int32)


def steps_of(key, shape, split, least, largest):
    def one(dim, shards_of):
        heights = jax.random.uniform(jax.random.fold_in(jax.random.fold_in(key, 6), dim), (shards_of,), jnp.float32, least / len(split), largest / len(split))
        return jnp.repeat(jnp.exp(heights), shape[dim] // shards_of).reshape((-1,) + (1,) * (len(shape) - dim - 1))

    level = one(*split[0])
    for cut in split[1:]:
        level = level * one(*cut)
    return level


def setup_inputs(seed: int = 0) -> dict:
    streams_of = jax.random.split(jax.random.key(seed), 7)
    kern_blocks = draw_kern_blocks(jax.random.fold_in(streams_of[6], 71), 0)
    kern_cols = draw_kern_cols(jax.random.fold_in(streams_of[6], 71), 0)
    state_kernel = draw_state_kernel(jax.random.fold_in(streams_of[6], 71), 0)
    start_v = jnp.clip(jnp.exp(math.log(5.0) - 2.3025851 * jax.random.uniform(streams_of[3], (N1, N2), jnp.float32) ** steps_of(streams_of[3], (N1, N2), ((0, 8), (1, 4)), -0.2, 0.2)), 0.5, 5.0)
    mu = jnp.clip(jnp.exp(math.log(2.0) - 2.3025851 * jax.random.uniform(streams_of[4], (N1, N2), jnp.float32) ** steps_of(streams_of[4], (N1, N2), ((0, 32),), -0.2, 0.2)), 0.2, 2.0)
    nu = jnp.clip(jnp.exp(math.log(2.0) - 2.3025851 * jax.random.uniform(streams_of[5], (N1, N2), jnp.float32) ** steps_of(streams_of[5], (N1, N2), ((0, 8), (1, 4)), -0.2, 0.2)), 0.2, 2.0)
    return dict(kern_blocks=kern_blocks, kern_cols=kern_cols, state_kernel=state_kernel, start_v=start_v, mu=mu, nu=nu)


def forward_mesh(kern_blocks, kern_cols, rounded_v):
    blocks = rounded_v.reshape(NB, B, N2)

    def one_row(pair):
        kern_row, col_row = pair
        picked = blocks[col_row].astype(jnp.float32)
        return jnp.einsum("kab,kbc->ac", kern_row.astype(jnp.float32), picked)

    return lax.map(one_row, (kern_blocks, kern_cols)).reshape(NB * B, N2)


def backward_mesh(kern_blocks, kern_cols, rounded_b):
    kern_dev = kern_blocks.reshape(N_MESH, NBR_DEV, DEG, B, B)
    cols_dev = kern_cols.reshape(N_MESH, NBR_DEV * DEG)
    rows_dev = rounded_b.reshape(N_MESH, NBR_DEV, B, N2)

    def add_device(total, triple):
        kern_part, col_part, row_part = triple
        spread = jnp.einsum("rkab,rac->rkbc", kern_part.astype(jnp.float32), row_part.astype(jnp.float32))
        partial_value = jax.ops.segment_sum(spread.reshape(NBR_DEV * DEG, B, N2), col_part, num_segments=NB)
        partial_value = lax.optimization_barrier(partial_value.astype(jnp.bfloat16)).astype(jnp.float32)
        return total + partial_value, None

    start = jnp.zeros((NB, B, N2), jnp.float32)
    total, _ = lax.scan(add_device, start, (kern_dev, cols_dev, rows_dev))
    return total.reshape(NB * B, N2)


def reference(kern_blocks, kern_cols, state_kernel, start_v, mu, nu):
    values = start_v
    potential_u = mu
    for sweep in range(ITERS):
        rounded_v = lax.optimization_barrier(values.astype(jnp.bfloat16))
        applied = forward_mesh(kern_blocks, kern_cols, rounded_v).astype(jnp.bfloat16)
        mixed = jnp.dot(applied, state_kernel.T, preferred_element_type=jnp.float32)
        potential_u = mu / mixed
        back_rows = jnp.dot(potential_u.astype(jnp.bfloat16), state_kernel, preferred_element_type=jnp.float32).astype(jnp.bfloat16)
        rounded_b = lax.optimization_barrier(back_rows)
        totals = backward_mesh(kern_blocks, kern_cols, rounded_b)
        values = nu / totals
    return potential_u, values
```

```python
import functools

import jax
import jax.numpy as jnp
from jax import lax
from jax.experimental import pallas as pl
from jax.experimental.pallas import tpu as pltpu
from jax.sharding import PartitionSpec as P

CAP_FAR = 2
ITERS = 2
CAP_NEAR = 6
MOST_SHIFTS = 8


VMEM = pl.BlockSpec(memory_space=pltpu.VMEM)
SMEM = pl.BlockSpec(memory_space=pltpu.SMEM)
ANY = pl.BlockSpec(memory_space=pl.ANY)
F32, BF16 = jnp.float32, jnp.bfloat16


def shifted(value, axis, steps):
    count = lax.axis_size(axis)
    return lax.ppermute(value, axis, [(i, (i + steps) % count) for i in range(count)])


def request_plan(owners, places, remote, peer_count, block_rows, width):
    peer_ids = jnp.arange(peer_count, dtype=jnp.int32)
    place_ids = jnp.arange(block_rows, dtype=jnp.int32)
    matches = (
        remote[:, None, None]
        & (owners[:, None, None] == peer_ids[None, :, None])
        & (places[:, None, None] == place_ids[None, None, :])
    )
    matches = matches.astype(jnp.int32)
    needed = jnp.max(matches, axis=0)
    ranking = jnp.cumsum(needed, axis=1) - needed
    ref_slots = jnp.sum(matches * ranking[None, :, :], axis=(1, 2))
    slot_ids = jnp.arange(width, dtype=jnp.int32)
    selected = needed[:, :, None] * (ranking[:, :, None] == slot_ids[None, None, :]).astype(
        jnp.int32
    )
    requests = jnp.sum(selected * place_ids[None, :, None], axis=1)
    return (ref_slots, requests)


class Plan:
    def __init__(self, kern_blocks, start_v):
        self.rows, self.degree, self.size, _ = kern_blocks.shape
        self.cols = start_v.shape[1]
        self.peers = lax.axis_size("mesh")
        self.states = lax.axis_size("state")
        self.near = CAP_NEAR
        self.far_base = self.rows + 2 * self.near
        self.table = self.far_base + self.peers * CAP_FAR
        self.share = self.rows // self.states
        self.chunks = 3 if self.share % 3 == 0 else 1
        self.group = self.share // self.chunks
        if self.peers <= MOST_SHIFTS:
            self.shifts = [d for d in range(2, self.peers - 1)]
        else:
            self.shifts = None

    def blocks(self, count, dtype):
        return jax.ShapeDtypeStruct((count, self.size, self.cols), dtype)

    def cost(self, matmul_blocks, nbytes):
        flops = 2 * matmul_blocks * self.size * self.size * self.cols
        return pl.CostEstimate(flops=flops, bytes_accessed=nbytes, transcendentals=0)


def forward_chunk(plan, chunk, where, sources, kern, own, left, right, far):
    n_far = len(far)
    group, states, degree = plan.group, plan.states, plan.degree

    def kernel(where_ref, src, kern_ref, own_ref, left_ref, right_ref, *rest):
        far_refs, outs = rest[:n_far], rest[n_far : n_far + states]
        tbl, kbuf, sem_t, sem_k = rest[n_far + states :]
        mine, me = where_ref[0], where_ref[1]
        pieces = [
            (left_ref, 0, plan.near),
            (own_ref, plan.near, plan.rows),
            (right_ref, plan.near + plan.rows, plan.near),
        ]
        if plan.shifts is None:
            pieces.append((far_refs[0], plan.far_base, plan.peers * CAP_FAR))
        else:
            for shift, ref in zip(plan.shifts, far_refs):
                owner = lax.rem(me - shift + plan.peers, plan.peers)
                pieces.append((ref, plan.far_base + CAP_FAR * owner, CAP_FAR))
        copies = [
            pltpu.make_async_copy(ref, tbl.at[pl.ds(at, count)], sem_t.at[i])
            for i, (ref, at, count) in enumerate(pieces)
        ]
        starts, loads = [], []
        for p in range(states):
            share = lax.rem(mine - p + states, states)
            starts.append(share * plan.share + chunk * group)
            loads.append(
                pltpu.make_async_copy(
                    kern_ref.at[pl.ds(starts[p], group)], kbuf.at[p], sem_k.at[p]
                )
            )
        loads[0].start()
        for copy in copies:
            copy.start()
        for load in loads[1:]:
            load.start()
        for copy in copies:
            copy.wait()
        for p in range(states):
            loads[p].wait()
            for g in range(group):
                base = (starts[p] + g) * degree
                lhs = jnp.concatenate([kbuf[p, g, k] for k in range(degree)], axis=1)
                rhs = jnp.concatenate([tbl[src[base + k]] for k in range(degree)], axis=0)
                out = jnp.dot(lhs, rhs, preferred_element_type=F32)
                outs[p][g] = out.astype(BF16)

    n_pieces = 3 + n_far
    return pl.pallas_call(
        kernel,
        name="forward",
        out_shape=[plan.blocks(group, BF16)] * states,
        in_specs=[SMEM, SMEM] + [ANY] * (4 + n_far),
        out_specs=[VMEM] * states,
        scratch_shapes=[
            pltpu.VMEM((plan.table, plan.size, plan.cols), BF16),
            pltpu.VMEM((states, group, degree, plan.size, plan.size), BF16),
            pltpu.SemaphoreType.DMA((n_pieces,)),
            pltpu.SemaphoreType.DMA((states,)),
        ],
        cost_estimate=plan.cost(states * group * degree, 6 << 20),
    )(where, sources, kern, own, left, right, *far)


def mix_chunk(plan, chunk, pieces, state_kernel, mu, u_so_far, emit_u):
    states, group = plan.states, plan.group
    height = group * plan.size

    def kernel(*refs):
        a_refs, (k_ref, mu_ref), rest = refs[:states], refs[states : states + 2], refs[states + 2 :]
        if emit_u and u_so_far is not None:
            rest = rest[1:]
        outs = rest[:states]
        for g in range(group):
            a = jnp.concatenate([ref[g] for ref in a_refs], axis=1)
            mixed = lax.dot_general(
                a, k_ref[...], (((1,), (1,)), ((), ())), preferred_element_type=F32
            )
            u = mu_ref[pl.ds(g * plan.size, plan.size), :] / mixed
            if emit_u:
                rest[states][pl.ds(g * plan.size, plan.size), :] = u
            b = jnp.dot(u.astype(BF16), k_ref[...], preferred_element_type=F32).astype(BF16)
            for p in range(states):
                outs[p][g] = b[:, p * plan.cols : (p + 1) * plan.cols]

    width = mu.shape[1]
    piece = pl.BlockSpec((group, plan.size, plan.cols), lambda i: (0, 0, 0))
    rows = pl.BlockSpec((height, width), lambda i: (chunk, 0))
    full = pl.BlockSpec((width, width), lambda i: (0, 0))
    args = list(pieces) + [state_kernel, mu]
    in_specs = [piece] * states + [full, rows]
    out_specs, out_shape, aliases = [piece] * states, [plan.blocks(group, BF16)] * states, {}
    if emit_u:
        out_specs = out_specs + [rows]
        out_shape = out_shape + [jax.ShapeDtypeStruct(mu.shape, F32)]
        if u_so_far is not None:
            args.append(u_so_far)
            in_specs.append(ANY)
            aliases = {len(args) - 1: states}
    out = pl.pallas_call(
        kernel,
        name="mix",
        grid=(1,),
        out_shape=out_shape,
        in_specs=in_specs,
        out_specs=out_specs,
        input_output_aliases=aliases,
        cost_estimate=plan.cost(2 * group * states * states, 3 << 20),
    )(*args)
    return (list(out[:states]), out[states] if emit_u else None)


def backward_chunk(plan, chunk, where, sources, kern, pieces, so_far):
    states, group, degree = plan.states, plan.group, plan.degree
    last = chunk == plan.chunks - 1
    n_far = len(plan.shifts) if plan.shifts is not None else 1
    n_acc = 0 if so_far is None else 1

    def kernel(where_ref, src, kern_ref, *rest):
        b_refs, rest = rest[:states], rest[states:]
        acc_refs, rest = rest[:n_acc], rest[n_acc:]
        n_out = 3 + n_far if last else 1
        outs, (acc, kbuf, sem_k), rest = rest[:n_out], rest[n_out : n_out + 3], rest[n_out + 3 :]
        mine, me = where_ref[0], where_ref[1]
        starts, loads = [], []
        for p in range(states):
            share = lax.rem(mine - p + states, states)
            starts.append(share * plan.share + chunk * group)
            load = pltpu.make_async_copy(
                kern_ref.at[pl.ds(starts[p], group)], kbuf.at[p], sem_k.at[p]
            )
            load.start()
            loads.append(load)
        if n_acc:
            earlier = pltpu.make_async_copy(acc_refs[0], rest[0], rest[1])
            earlier.start()
        acc[...] = jnp.zeros_like(acc)
        for p in range(states):
            loads[p].wait()
            for g in range(group):
                base = (starts[p] + g) * degree
                b = b_refs[p][g]
                for k in range(degree):
                    part = lax.dot_general(
                        kbuf[p, g, k], b, (((0,), (0,)), ((), ())), preferred_element_type=F32
                    )
                    acc[src[base + k]] += part
        if n_acc:
            earlier.wait()

        def total(at):
            if n_acc:
                return acc[at] + rest[0][at]
            return acc[at]

        if not last:
            for t in range(plan.table):
                outs[0][t] = total(t)
            return
        own, left, right, far = outs[0], outs[1], outs[2], outs[3:]
        for t in range(plan.near):
            left[t] = total(t).astype(BF16)
            right[t] = total(plan.near + plan.rows + t).astype(BF16)
        for t in range(plan.rows):
            own[t] = total(plan.near + t)
        if plan.shifts is None:
            for t in range(plan.peers * CAP_FAR):
                far[0][t] = total(plan.far_base + t).astype(BF16)
        else:
            for shift, ref in zip(plan.shifts, far):
                owner = lax.rem(me + shift, plan.peers)
                for t in range(CAP_FAR):
                    ref[t] = total(plan.far_base + CAP_FAR * owner + t).astype(BF16)

    if last:
        far_count = CAP_FAR if plan.shifts is not None else plan.peers * CAP_FAR
        out_shape = [plan.blocks(plan.rows, F32)] + [plan.blocks(plan.near, BF16)] * 2
        out_shape += [plan.blocks(far_count, BF16)] * n_far
    else:
        out_shape = [plan.blocks(plan.table, F32)]
    acc_shape = pltpu.VMEM((plan.table, plan.size, plan.cols), F32)
    scratch = [
        acc_shape,
        pltpu.VMEM((states, group, degree, plan.size, plan.size), BF16),
        pltpu.SemaphoreType.DMA((states,)),
    ]
    if n_acc:
        scratch += [acc_shape, pltpu.SemaphoreType.DMA]
    return pl.pallas_call(
        kernel,
        name="backward",
        out_shape=out_shape,
        in_specs=[SMEM, SMEM, ANY] + [VMEM] * states + [ANY] * n_acc,
        out_specs=[VMEM] * len(out_shape),
        scratch_shapes=scratch,
        cost_estimate=plan.cost(states * group * degree, 10 << 20),
    )(where, sources, kern, *pieces, *([] if so_far is None else [so_far]))


def far_owner(plan, me, shift):
    return lax.rem(me + shift + plan.peers, plan.peers)


def emit_far(plan, me, asked, source, outs):
    if plan.shifts is None:
        for t in range(plan.peers * CAP_FAR):
            outs[0][t] = source[asked[t]]
    else:
        for shift, ref in zip(plan.shifts, outs):
            peer = far_owner(plan, me, shift)
            for t in range(CAP_FAR):
                ref[t] = source[asked[peer * CAP_FAR + t]]


def far_shapes(plan):
    if plan.shifts is None:
        return [plan.blocks(plan.peers * CAP_FAR, BF16)]
    return [plan.blocks(CAP_FAR, BF16)] * len(plan.shifts)


def far_blocks(plan, where, asked, own):
    def kernel(where_ref, asked_ref, own_ref, *outs):
        emit_far(plan, where_ref[1], asked_ref, own_ref, outs)

    shapes = far_shapes(plan)
    return pl.pallas_call(
        kernel,
        name="far_blocks",
        out_shape=shapes,
        in_specs=[SMEM, SMEM, VMEM],
        out_specs=[VMEM] * len(shapes),
        cost_estimate=plan.cost(0, 2 << 20),
    )(where, asked, own)


def divide(plan, where, asked, own, from_right, from_left, arrived, nu, final):
    n_far = len(arrived)

    def kernel(where_ref, asked_ref, own_ref, right_ref, left_ref, *rest):
        far_refs, (nu_ref,), rest = rest[:n_far], rest[n_far : n_far + 1], rest[n_far + 1 :]
        outs, acc = rest[:-1], rest[-1]
        me = where_ref[1]
        for t in range(plan.rows):
            value = own_ref[t]
            if t < plan.near:
                value = value + left_ref[t].astype(F32)
            if t >= plan.rows - plan.near:
                value = value + right_ref[t - plan.rows + plan.near].astype(F32)
            acc[t] = value
        if plan.shifts is None:
            for t in range(plan.peers * CAP_FAR):
                acc[asked_ref[t]] += far_refs[0][t].astype(F32)
        else:
            for shift, ref in zip(plan.shifts, far_refs):
                peer = far_owner(plan, me, -shift)
                for t in range(CAP_FAR):
                    acc[asked_ref[peer * CAP_FAR + t]] += ref[t].astype(F32)
        for t in range(plan.rows):
            value = nu_ref[t] / acc[t]
            if final:
                outs[0][t] = value
            else:
                value = value.astype(BF16)
                outs[0][t] = value
                if t < plan.near:
                    outs[1][t] = value
                if t >= plan.rows - plan.near:
                    outs[2][t - plan.rows + plan.near] = value
        if not final:
            emit_far(plan, me, asked_ref, outs[0], outs[3:])

    if final:
        out_shape = [plan.blocks(plan.rows, F32)]
    else:
        out_shape = [plan.blocks(plan.rows, BF16)] + [plan.blocks(plan.near, BF16)] * 2
        out_shape += far_shapes(plan)
    return pl.pallas_call(
        kernel,
        name="divide",
        out_shape=out_shape,
        in_specs=[SMEM, SMEM] + [VMEM] * (4 + n_far),
        out_specs=[VMEM] * len(out_shape),
        scratch_shapes=[pltpu.VMEM((plan.rows, plan.size, plan.cols), F32)],
        cost_estimate=plan.cost(0, 6 << 20),
    )(where, asked, own, from_right, from_left, *arrived, nu)


def send_far(plan, pieces):
    if plan.shifts is None:
        return [lax.all_to_all(pieces[0], "mesh", split_axis=0, concat_axis=0, tiled=True)]
    return [shifted(piece, "mesh", d) for d, piece in zip(plan.shifts, pieces)]


def per_device(kern_blocks, kern_cols, state_kernel, start_v, mu, nu):
    plan = Plan(kern_blocks, start_v)
    me, mine = lax.axis_index("mesh"), lax.axis_index("state")
    where = jnp.stack([mine, me]).astype(jnp.int32)
    left_index = (me + plan.peers - 1) % plan.peers
    right_index = (me + 1) % plan.peers
    flat_cols = kern_cols.reshape(-1)
    owners = flat_cols // plan.rows
    places = flat_cols % plan.rows
    near_source = jnp.where(
        owners == left_index,
        places - (plan.rows - plan.near),
        jnp.where(owners == right_index, plan.near + plan.rows + places, plan.near + places),
    )
    remote = (owners != me) & (owners != left_index) & (owners != right_index)
    ref_slots, requests = request_plan(owners, places, remote, plan.peers, plan.rows, CAP_FAR)
    asked = lax.all_to_all(requests, "mesh", split_axis=0, concat_axis=0, tiled=True).reshape(-1)
    sources = jnp.where(remote, plan.far_base + owners * CAP_FAR + ref_slots, near_source)
    width = state_kernel.shape[0]
    turned = lax.dynamic_slice_in_dim(
        jnp.concatenate([state_kernel, state_kernel], axis=1), mine * plan.cols, width, axis=1
    )

    own = start_v.astype(BF16).reshape(plan.rows, plan.size, plan.cols)
    nu = nu.reshape(plan.rows, plan.size, plan.cols)
    head, tail = own[: plan.near], own[plan.rows - plan.near :]
    far_out = far_blocks(plan, where, asked, own)
    potential_u = None
    for sweep in range(ITERS):
        final = sweep == ITERS - 1
        from_left, from_right = shifted(tail, "mesh", 1), shifted(head, "mesh", -1)
        far_in = send_far(plan, far_out)
        spread = []
        for c in range(plan.chunks):
            parts = forward_chunk(
                plan, c, where, sources, kern_blocks, own, from_left, from_right, far_in
            )
            spread.append(
                [parts[0]] + [shifted(parts[p], "state", -p) for p in range(1, plan.states)]
            )
        returned = []
        for c in range(plan.chunks):
            parts, potential_u = mix_chunk(plan, c, spread[c], turned, mu, potential_u, final)
            returned.append(
                [parts[0]] + [shifted(parts[p], "state", p) for p in range(1, plan.states)]
            )
        total = None
        for c in range(plan.chunks):
            out = backward_chunk(plan, c, where, sources, kern_blocks, returned[c], total)
            total = out[0]
        own_part, to_left, to_right, far_parts = out[0], out[1], out[2], out[3:]
        from_right, from_left = shifted(to_left, "mesh", -1), shifted(to_right, "mesh", 1)
        arrived = send_far(plan, far_parts)
        out = divide(plan, where, asked, own_part, from_right, from_left, arrived, nu, final)
        if final:
            values = out[0]
        else:
            own, head, tail, far_out = out[0], out[1], out[2], out[3:]
    return (potential_u, values.reshape(start_v.shape))


def solution(mesh):
    placed = (
        P("mesh", None, None, None),
        P("mesh", None),
        P(),
        P("mesh", "state"),
        P(("mesh", "state"), None),
        P("mesh", "state"),
    )
    return jax.shard_map(
        per_device,
        mesh=mesh,
        in_specs=placed,
        out_specs=(P(("mesh", "state"), None), P("mesh", "state")),
        check_vma=False,
    )
```

```python
import functools

import jax
import jax.numpy as jnp
from jax import lax
from jax.experimental import pallas as pl
from jax.experimental.pallas import tpu as pltpu
from jax.sharding import PartitionSpec as P

CAP_FAR = 2
ITERS = 2
CAP_NEAR = 6


VMEM = pl.BlockSpec(memory_space=pltpu.VMEM)
SMEM = pl.BlockSpec(memory_space=pltpu.SMEM)
ANY = pl.BlockSpec(memory_space=pl.ANY)
PARAMS = pltpu.CompilerParams(vmem_limit_bytes=16 << 20)
F32, BF16 = jnp.float32, jnp.bfloat16
CHUNKS = 2


def here(value):
    return pltpu.with_memory_space_constraint(value, pltpu.VMEM)


def shifted(value, axis, steps):
    count = lax.axis_size(axis)
    return lax.ppermute(value, axis, [(i, (i + steps) % count) for i in range(count)])


def swapped(value, axis):
    return lax.all_to_all(value, axis, split_axis=0, concat_axis=0, tiled=True)


def request_plan(owners, places, remote, peer_count, block_rows, width):
    peer_ids = jnp.arange(peer_count, dtype=jnp.int32)
    place_ids = jnp.arange(block_rows, dtype=jnp.int32)
    matches = (
        remote[:, None, None]
        & (owners[:, None, None] == peer_ids[None, :, None])
        & (places[:, None, None] == place_ids[None, None, :])
    )
    matches = matches.astype(jnp.int32)
    needed = jnp.max(matches, axis=0)
    ranking = jnp.cumsum(needed, axis=1) - needed
    ref_slots = jnp.sum(matches * ranking[None, :, :], axis=(1, 2))
    slot_ids = jnp.arange(width, dtype=jnp.int32)
    selected = needed[:, :, None] * (ranking[:, :, None] == slot_ids[None, None, :]).astype(
        jnp.int32
    )
    requests = jnp.sum(selected * place_ids[None, :, None], axis=1)
    return (ref_slots, requests)


class Plan:
    def __init__(self, kern_blocks, start_v):
        self.rows, self.degree, self.size, _ = kern_blocks.shape
        self.cols = start_v.shape[1]
        self.peers = lax.axis_size("mesh")
        self.states = lax.axis_size("state")
        self.near, self.far = CAP_NEAR, CAP_FAR
        self.edge = self.near - self.far
        self.far_base = self.rows + 2 * self.near
        self.table = self.far_base + self.peers * self.far
        self.share = self.rows // self.states
        self.chunks = CHUNKS if self.share % CHUNKS == 0 else 1
        self.group = self.share // self.chunks

    def blocks(self, count, dtype):
        return pltpu.VMEM((count, self.size, self.cols), dtype)

    def pieces(self):
        return pltpu.VMEM((self.states, self.group, self.size, self.cols), BF16)

    def cost(self, matmul_blocks, nbytes):
        flops = 2 * matmul_blocks * self.size * self.size * self.cols
        return pl.CostEstimate(flops=flops, bytes_accessed=nbytes, transcendentals=0)


def call(kernel, name, out_shape, in_specs, args, cost, scratch=(), aliases={}, out_specs=None):
    args = [here(a) if spec is VMEM else a for spec, a in zip(in_specs, args)]
    return pl.pallas_call(
        kernel,
        name=name,
        out_shape=out_shape,
        in_specs=in_specs,
        out_specs=[VMEM] * len(out_shape) if out_specs is None else out_specs,
        scratch_shapes=list(scratch),
        input_output_aliases=aliases,
        compiler_params=PARAMS,
        cost_estimate=cost,
    )(*args)


def forward_chunk(plan, chunk, where, sources, kern, own, left, right, others):
    group, states, degree, edge, far = plan.group, plan.states, plan.degree, plan.edge, plan.far

    def kernel(where_ref, src, kern_ref, own_ref, left_ref, right_ref, other_ref, out, tbl):
        me = where_ref[1]
        before = lax.rem(me + plan.peers - 1, plan.peers) * far
        after = lax.rem(me + 1, plan.peers) * far
        after_base = plan.near + plan.rows
        for t in range(edge):
            tbl[t] = left_ref[t]
            tbl[after_base + far + t] = right_ref[t]
        for t in range(far):
            tbl[edge + t] = other_ref[before + t]
            tbl[after_base + t] = other_ref[after + t]
        for t in range(plan.rows):
            tbl[plan.near + t] = own_ref[t]
        for t in range(plan.peers * far):
            tbl[plan.far_base + t] = other_ref[t]
        for p in range(states):
            for g in range(group):
                row = p * plan.share + chunk * group + g
                lhs = jnp.concatenate([kern_ref[row, k] for k in range(degree)], axis=1)
                rhs = jnp.concatenate(
                    [tbl[src[row * degree + k]] for k in range(degree)], axis=0
                )
                out[p, g] = jnp.dot(lhs, rhs, preferred_element_type=F32).astype(BF16)

    return call(
        kernel,
        "forward",
        [plan.pieces()],
        [SMEM, SMEM] + [VMEM] * 5,
        [where, sources, kern, own, left, right, others],
        plan.cost(states * group * degree, 6 << 20),
        [pltpu.VMEM((plan.table, plan.size, plan.cols), BF16)],
    )[0]


def mix_chunk(plan, chunk, pieces, state_kernel, mu, u_so_far, emit_u):
    states, group, size = plan.states, plan.group, plan.size
    height = group * size
    passed = emit_u and u_so_far is not None

    def kernel(a_ref, k_ref, mu_ref, *rest):
        if passed:
            rest = rest[1:]
        out = rest[0]
        copies = []
        for g in range(group):
            a = jnp.concatenate([a_ref[p, g] for p in range(states)], axis=1)
            mixed = lax.dot_general(
                a, k_ref[...], (((1,), (1,)), ((), ())), preferred_element_type=F32
            )
            at = chunk * height + g * size
            u = mu_ref[pl.ds(at, size), :] / mixed
            if emit_u:
                u_ref, u_buf, sem = rest[1:]
                u_buf[g] = u
                copy = pltpu.make_async_copy(u_buf.at[g], u_ref.at[pl.ds(at, size), :], sem.at[g])
                copy.start()
                copies.append(copy)
            b = jnp.dot(u.astype(BF16), k_ref[...], preferred_element_type=F32).astype(BF16)
            for p in range(states):
                out[p, g] = b[:, p * plan.cols : (p + 1) * plan.cols]
        for copy in copies:
            copy.wait()

    args, in_specs = [pieces, state_kernel, mu], [VMEM] * 3
    out_shape, out_specs, scratch, aliases = [plan.pieces()], [VMEM], [], {}
    if emit_u:
        out_shape.append(jax.ShapeDtypeStruct(mu.shape, F32))
        out_specs.append(ANY)
        scratch = [pltpu.VMEM((group, size, mu.shape[1]), F32), pltpu.SemaphoreType.DMA((group,))]
        if passed:
            args.append(u_so_far)
            in_specs.append(ANY)
            aliases = {3: 1}
    out = call(
        kernel,
        "mix",
        out_shape,
        in_specs,
        args,
        plan.cost(2 * group * states * states, 3 << 20),
        scratch,
        aliases,
        out_specs,
    )
    return (out[0], out[1] if emit_u else None)


def backward_chunk(plan, chunk, where, sources, kern, pieces, so_far):
    states, group, degree = plan.states, plan.group, plan.degree
    edge, far = plan.edge, plan.far
    last = chunk == plan.chunks - 1
    n_acc = 0 if so_far is None else 1

    def kernel(where_ref, src, kern_ref, b_ref, *rest):
        rest = rest[n_acc:]
        acc = rest[-1]
        if not n_acc:
            acc[...] = jnp.zeros_like(acc)
        if last and n_acc:
            pass
        for p in range(states):
            for g in range(group):
                row = p * plan.share + chunk * group + g
                b = b_ref[p, g]
                for k in range(degree):
                    part = lax.dot_general(
                        kern_ref[row, k], b, (((0,), (0,)), ((), ())), preferred_element_type=F32
                    )
                    acc[src[row * degree + k]] += part
        if not last:
            return
        own, left, right, others = rest[:4]
        me = where_ref[1]
        before = lax.rem(me + plan.peers - 1, plan.peers) * far
        after = lax.rem(me + 1, plan.peers) * far
        after_base = plan.near + plan.rows
        for t in range(plan.rows):
            own[t] = acc[plan.near + t].astype(BF16)
        for t in range(plan.peers * far):
            others[t] = acc[plan.far_base + t].astype(BF16)
        for t in range(edge):
            left[t] = acc[t].astype(BF16)
            right[t] = acc[after_base + far + t].astype(BF16)
        for t in range(far):
            others[before + t] = acc[edge + t].astype(BF16)
            others[after + t] = acc[after_base + t].astype(BF16)

    acc_shape = plan.blocks(plan.table, F32)
    if last:
        out_shape = [plan.blocks(n, BF16) for n in (plan.rows, edge, edge, plan.peers * far)]
    else:
        out_shape = []
    return call(
        kernel,
        "backward",
        out_shape + [acc_shape],
        [SMEM, SMEM, VMEM, VMEM] + [VMEM] * n_acc,
        [where, sources, kern, pieces] + ([] if so_far is None else [so_far]),
        plan.cost(states * group * degree, 10 << 20),
        (),
        {4: len(out_shape)} if n_acc else {},
    )


def emit_others(plan, me, asked, source, out):
    before = lax.rem(me + plan.peers - 1, plan.peers) * plan.far
    after = lax.rem(me + 1, plan.peers) * plan.far
    for t in range(plan.peers * plan.far):
        out[t] = source[asked[t]]
    for t in range(plan.far):
        out[before + t] = source[t]
        out[after + t] = source[plan.rows - plan.far + t]


def first_others(plan, where, asked, own):
    def kernel(where_ref, asked_ref, own_ref, out):
        emit_others(plan, where_ref[1], asked_ref, own_ref, out)

    return call(
        kernel,
        "others",
        [plan.blocks(plan.peers * plan.far, BF16)],
        [SMEM, SMEM, VMEM],
        [where, asked, own],
        plan.cost(0, 2 << 20),
    )[0]


def divide(plan, where, asked, own, from_right, from_left, arrived, nu, final):
    near, far, edge, rows = plan.near, plan.far, plan.edge, plan.rows

    def kernel(where_ref, asked_ref, own_ref, right_ref, left_ref, other_ref, nu_ref, *rest):
        outs, acc = rest[:-1], rest[-1]
        me = where_ref[1]
        before = lax.rem(me + plan.peers - 1, plan.peers) * far
        after = lax.rem(me + 1, plan.peers) * far
        for t in range(rows):
            value = own_ref[t].astype(F32)
            if t < far:
                value = value + other_ref[before + t].astype(F32)
            elif t < near:
                value = value + left_ref[t - far].astype(F32)
            if t >= rows - far:
                value = value + other_ref[after + t - rows + far].astype(F32)
            elif t >= rows - near:
                value = value + right_ref[t - rows + near].astype(F32)
            acc[t] = value
        for p in range(plan.peers):
            beside = (p * far == before) | (p * far == after)

            @pl.when(jnp.logical_not(beside))
            def _():
                for t in range(p * far, p * far + far):
                    acc[asked_ref[t]] += other_ref[t].astype(F32)

        for t in range(rows):
            value = nu_ref[t] / acc[t]
            if final:
                outs[0][t] = value
            else:
                value = value.astype(BF16)
                outs[0][t] = value
                if far <= t < near:
                    outs[1][t - far] = value
                if rows - near <= t < rows - far:
                    outs[2][t - rows + near] = value
        if not final:
            emit_others(plan, me, asked_ref, outs[0], outs[3])

    if final:
        out_shape = [jax.ShapeDtypeStruct((rows, plan.size, plan.cols), F32)]
    else:
        out_shape = [plan.blocks(n, BF16) for n in (rows, edge, edge, plan.peers * far)]
    return call(
        kernel,
        "divide",
        out_shape,
        [SMEM, SMEM] + [VMEM] * 5,
        [where, asked, own, from_right, from_left, arrived, nu],
        plan.cost(0, 6 << 20),
        [pltpu.VMEM((rows, plan.size, plan.cols), F32)],
    )


def per_device(kern_blocks, kern_cols, state_kernel, start_v, mu, nu):
    plan = Plan(kern_blocks, start_v)
    me, mine = lax.axis_index("mesh"), lax.axis_index("state")
    where = jnp.stack([mine, me]).astype(jnp.int32)
    left_index = (me + plan.peers - 1) % plan.peers
    right_index = (me + 1) % plan.peers
    flat_cols = kern_cols.reshape(-1)
    owners = flat_cols // plan.rows
    places = flat_cols % plan.rows
    near_source = jnp.where(
        owners == left_index,
        places - (plan.rows - plan.near),
        jnp.where(owners == right_index, plan.near + plan.rows + places, plan.near + places),
    )
    remote = (owners != me) & (owners != left_index) & (owners != right_index)
    ref_slots, requests = request_plan(owners, places, remote, plan.peers, plan.rows, CAP_FAR)
    asked = swapped(requests, "mesh").reshape(-1)
    sources = jnp.where(remote, plan.far_base + owners * CAP_FAR + ref_slots, near_source)

    own = start_v.astype(BF16).reshape(plan.rows, plan.size, plan.cols)
    nu = nu.reshape(plan.rows, plan.size, plan.cols)
    head = own[plan.far : plan.near]
    tail = own[plan.rows - plan.near : plan.rows - plan.far]
    others = first_others(plan, where, asked, own)
    kern, state_kernel, nu, mu = here(kern_blocks), here(state_kernel), here(nu), here(mu)
    potential_u = None
    for sweep in range(ITERS):
        final = sweep == ITERS - 1
        from_left, from_right = shifted(tail, "mesh", 1), shifted(head, "mesh", -1)
        others = swapped(others, "mesh")
        spread = []
        for c in range(plan.chunks):
            part = forward_chunk(
                plan, c, where, sources, kern, own, from_left, from_right, others
            )
            spread.append(swapped(part, "state"))
        returned = []
        for c in range(plan.chunks):
            part, potential_u = mix_chunk(plan, c, spread[c], state_kernel, mu, potential_u, final)
            returned.append(swapped(part, "state"))
        total = None
        for c in range(plan.chunks):
            out = backward_chunk(plan, c, where, sources, kern, returned[c], total)
            total = out[-1]
        own_part, to_left, to_right, to_others = out[:4]
        from_right, from_left = shifted(to_left, "mesh", -1), shifted(to_right, "mesh", 1)
        arrived = swapped(to_others, "mesh")
        out = divide(plan, where, asked, own_part, from_right, from_left, arrived, nu, final)
        if final:
            values = out[0]
        else:
            own, head, tail, others = out
    return (potential_u, values.reshape(start_v.shape))


def solution(mesh):
    placed = (
        P("mesh", None, None, None),
        P("mesh", None),
        P(),
        P("mesh", "state"),
        P(("mesh", "state"), None),
        P("mesh", "state"),
    )
    return jax.shard_map(
        per_device,
        mesh=mesh,
        in_specs=placed,
        out_specs=(P(("mesh", "state"), None), P("mesh", "state")),
        check_vma=False,
    )
```

```python
import functools

import jax
import jax.numpy as jnp
from jax import lax
from jax.experimental import pallas as pl
from jax.experimental.pallas import tpu as pltpu
from jax.sharding import PartitionSpec as P

CAP_FAR = 2
ITERS = 2
CAP_NEAR = 6


VMEM = pl.BlockSpec(memory_space=pltpu.VMEM)
SMEM = pl.BlockSpec(memory_space=pltpu.SMEM)
ANY = pl.BlockSpec(memory_space=pl.ANY)
PARAMS = pltpu.CompilerParams(vmem_limit_bytes=16 << 20)
F32, BF16 = jnp.float32, jnp.bfloat16
CHUNKS = 2
MOST_SHIFTS = 8


def here(value):
    return pltpu.with_memory_space_constraint(value, pltpu.VMEM)


def shifted(value, axis, steps):
    count = lax.axis_size(axis)
    return lax.ppermute(value, axis, [(i, (i + steps) % count) for i in range(count)])


def swapped(value, axis):
    return lax.all_to_all(value, axis, split_axis=0, concat_axis=0, tiled=True)


def request_plan(owners, places, remote, peer_count, block_rows, width):
    peer_ids = jnp.arange(peer_count, dtype=jnp.int32)
    place_ids = jnp.arange(block_rows, dtype=jnp.int32)
    matches = (
        remote[:, None, None]
        & (owners[:, None, None] == peer_ids[None, :, None])
        & (places[:, None, None] == place_ids[None, None, :])
    )
    matches = matches.astype(jnp.int32)
    needed = jnp.max(matches, axis=0)
    ranking = jnp.cumsum(needed, axis=1) - needed
    ref_slots = jnp.sum(matches * ranking[None, :, :], axis=(1, 2))
    slot_ids = jnp.arange(width, dtype=jnp.int32)
    selected = needed[:, :, None] * (ranking[:, :, None] == slot_ids[None, None, :]).astype(
        jnp.int32
    )
    requests = jnp.sum(selected * place_ids[None, :, None], axis=1)
    return (ref_slots, requests)


class Plan:
    def __init__(self, kern_blocks, start_v):
        self.rows, self.degree, self.size, _ = kern_blocks.shape
        self.cols = start_v.shape[1]
        self.peers = lax.axis_size("mesh")
        self.states = lax.axis_size("state")
        self.near, self.far = CAP_NEAR, CAP_FAR
        self.far_base = self.rows + 2 * self.near
        self.table = self.far_base + self.peers * self.far
        self.share = self.rows // self.states
        self.chunks = CHUNKS if self.share % CHUNKS == 0 else 1
        self.group = self.share // self.chunks
        self.shifts = range(2, self.peers - 1) if self.peers <= MOST_SHIFTS else None

    def blocks(self, count, dtype):
        return pltpu.VMEM((count, self.size, self.cols), dtype)

    def far_blocks(self):
        if self.shifts is None:
            return [self.blocks(self.peers * self.far, BF16)]
        return [self.blocks(self.far, BF16)] * len(self.shifts)

    def far_slots(self, me, refs, way):
        if self.shifts is None:
            return [(t, refs[0], t) for t in range(self.peers * self.far)]
        slots = []
        for shift, ref in zip(self.shifts, refs):
            peer = lax.rem(me + way * shift + self.peers, self.peers)
            slots += [(peer * self.far + t, ref, t) for t in range(self.far)]
        return slots

    def cost(self, matmul_blocks, nbytes):
        flops = 2 * matmul_blocks * self.size * self.size * self.cols
        return pl.CostEstimate(flops=flops, bytes_accessed=nbytes, transcendentals=0)

    def rows_of(self, state, p, chunk):
        return lax.rem(state - p + self.states, self.states) * self.share + chunk * self.group


def call(kernel, name, out_shape, in_specs, args, cost, scratch=(), aliases={}, out_specs=None):
    args = [here(a) if spec is VMEM else a for spec, a in zip(in_specs, args)]
    return pl.pallas_call(
        kernel,
        name=name,
        out_shape=out_shape,
        in_specs=in_specs,
        out_specs=[VMEM] * len(out_shape) if out_specs is None else out_specs,
        scratch_shapes=list(scratch),
        input_output_aliases=aliases,
        compiler_params=PARAMS,
        cost_estimate=cost,
    )(*args)


def forward_chunk(plan, chunk, where, sources, kern, own, left, right, far):
    group, states, degree, near = plan.group, plan.states, plan.degree, plan.near
    n_far = len(far)

    def kernel(where_ref, src, kern_ref, own_ref, left_ref, right_ref, *rest):
        far_refs, outs, tbl = rest[:n_far], rest[n_far:-1], rest[-1]
        for t in range(near):
            tbl[t] = left_ref[t]
            tbl[near + plan.rows + t] = right_ref[t]
        for t in range(plan.rows):
            tbl[near + t] = own_ref[t]
        for slot, ref, t in plan.far_slots(where_ref[1], far_refs, -1):
            tbl[plan.far_base + slot] = ref[t]
        for p in range(states):
            first = plan.rows_of(where_ref[0], p, chunk)
            for g in range(group):
                row = first + g
                lhs = jnp.concatenate([kern_ref[row, k] for k in range(degree)], axis=1)
                rhs = jnp.concatenate(
                    [tbl[src[row * degree + k]] for k in range(degree)], axis=0
                )
                outs[p][g] = jnp.dot(lhs, rhs, preferred_element_type=F32).astype(BF16)

    return call(
        kernel,
        "forward",
        [plan.blocks(group, BF16)] * states,
        [SMEM, SMEM] + [VMEM] * (4 + n_far),
        [where, sources, kern, own, left, right, *far],
        plan.cost(states * group * degree, 6 << 20),
        [pltpu.VMEM((plan.table, plan.size, plan.cols), BF16)],
    )


def mix_chunk(plan, chunk, where, pieces, state_kernel, mu, u_so_far, emit_u):
    states, group, size, cols = plan.states, plan.group, plan.size, plan.cols
    height = group * size
    passed = emit_u and u_so_far is not None

    def kernel(where_ref, *refs):
        a_refs, (k_ref, mu_ref), rest = refs[:states], refs[states : states + 2], refs[states + 2 :]
        if passed:
            rest = rest[1:]
        outs, rest = rest[:states], rest[states:]
        turned = []
        for p in range(states):
            at = pl.multiple_of(lax.rem(where_ref[0] + p, states) * cols, cols)
            turned.append(k_ref[:, pl.ds(at, cols)])
        turned = jnp.concatenate(turned, axis=1)
        copies = []
        for g in range(group):
            a = jnp.concatenate([ref[g] for ref in a_refs], axis=1)
            mixed = lax.dot_general(
                a, turned, (((1,), (1,)), ((), ())), preferred_element_type=F32
            )
            at = chunk * height + g * size
            u = mu_ref[pl.ds(at, size), :] / mixed
            if emit_u:
                u_ref, u_buf, sem = rest
                u_buf[g] = u
                copy = pltpu.make_async_copy(u_buf.at[g], u_ref.at[pl.ds(at, size), :], sem.at[g])
                copy.start()
                copies.append(copy)
            b = jnp.dot(u.astype(BF16), turned, preferred_element_type=F32).astype(BF16)
            for p in range(states):
                outs[p][g] = b[:, p * cols : (p + 1) * cols]
        for copy in copies:
            copy.wait()

    args, in_specs = [where, *pieces, state_kernel, mu], [SMEM] + [VMEM] * (states + 2)
    out_shape = [plan.blocks(group, BF16)] * states
    out_specs, scratch, aliases = [VMEM] * states, [], {}
    if emit_u:
        out_shape = out_shape + [jax.ShapeDtypeStruct(mu.shape, F32)]
        out_specs = out_specs + [ANY]
        scratch = [pltpu.VMEM((group, size, mu.shape[1]), F32), pltpu.SemaphoreType.DMA((group,))]
        if passed:
            aliases = {len(args): states}
            args.append(u_so_far)
            in_specs.append(ANY)
    out = call(
        kernel,
        "mix",
        out_shape,
        in_specs,
        args,
        plan.cost(2 * group * states * states, 3 << 20),
        scratch,
        aliases,
        out_specs,
    )
    return (out[:states], out[states] if emit_u else None)


def backward_chunk(plan, chunk, where, sources, kern, pieces, so_far):
    states, group, degree, near = plan.states, plan.group, plan.degree, plan.near
    last = chunk == plan.chunks - 1
    n_acc = 0 if so_far is None else 1

    def kernel(where_ref, src, kern_ref, *rest):
        b_refs, rest = rest[:states], rest[states + n_acc :]
        acc = rest[-1]
        if not n_acc:
            acc[...] = jnp.zeros_like(acc)
        for p in range(states):
            first = plan.rows_of(where_ref[0], p, chunk)
            for g in range(group):
                row = first + g
                b = b_refs[p][g]
                for k in range(degree):
                    part = lax.dot_general(
                        kern_ref[row, k], b, (((0,), (0,)), ((), ())), preferred_element_type=F32
                    )
                    acc[src[row * degree + k]] += part
        if not last:
            return
        own, left, right, far = rest[0], rest[1], rest[2], rest[3:-1]
        for t in range(near):
            left[t] = acc[t].astype(BF16)
            right[t] = acc[near + plan.rows + t].astype(BF16)
        for slot, ref, t in plan.far_slots(where_ref[1], far, 1):
            ref[t] = acc[plan.far_base + slot].astype(BF16)
        for t in range(plan.rows):
            own[t] = acc[near + t].astype(BF16)

    out_shape = []
    if last:
        out_shape = [plan.blocks(n, BF16) for n in (plan.rows, near, near)] + plan.far_blocks()
    return call(
        kernel,
        "backward",
        out_shape + [plan.blocks(plan.table, F32)],
        [SMEM, SMEM] + [VMEM] * (1 + states + n_acc),
        [where, sources, kern, *pieces] + ([] if so_far is None else [so_far]),
        plan.cost(states * group * degree, 10 << 20),
        (),
        {3 + states: len(out_shape)} if n_acc else {},
    )


def first_far(plan, where, asked, own):
    def kernel(where_ref, asked_ref, own_ref, *outs):
        for slot, ref, t in plan.far_slots(where_ref[1], outs, 1):
            ref[t] = own_ref[asked_ref[slot]]

    return call(
        kernel,
        "first_far",
        plan.far_blocks(),
        [SMEM, SMEM, VMEM],
        [where, asked, own],
        plan.cost(0, 2 << 20),
    )


def divide(plan, where, asked, own, from_right, from_left, arrived, nu, final):
    near, rows, n_far = plan.near, plan.rows, len(arrived)

    def kernel(where_ref, asked_ref, own_ref, right_ref, left_ref, *rest):
        far_refs, nu_ref, outs, acc = rest[:n_far], rest[n_far], rest[n_far + 1 : -1], rest[-1]
        for t in range(rows):
            value = own_ref[t].astype(F32)
            if t < near:
                value = value + left_ref[t].astype(F32)
            if t >= rows - near:
                value = value + right_ref[t - rows + near].astype(F32)
            acc[t] = value
        for slot, ref, t in plan.far_slots(where_ref[1], far_refs, -1):
            acc[asked_ref[slot]] += ref[t].astype(F32)
        for t in range(rows):
            value = nu_ref[t] / acc[t]
            if final:
                outs[0][t] = value
            else:
                value = value.astype(BF16)
                outs[0][t] = value
                if t < near:
                    outs[1][t] = value
                if t >= rows - near:
                    outs[2][t - rows + near] = value
        if not final:
            for slot, ref, t in plan.far_slots(where_ref[1], outs[3:], 1):
                ref[t] = outs[0][asked_ref[slot]]

    if final:
        out_shape = [jax.ShapeDtypeStruct((rows, plan.size, plan.cols), F32)]
    else:
        out_shape = [plan.blocks(n, BF16) for n in (rows, near, near)] + plan.far_blocks()
    return call(
        kernel,
        "divide",
        out_shape,
        [SMEM, SMEM] + [VMEM] * (4 + n_far),
        [where, asked, own, from_right, from_left, *arrived, nu],
        plan.cost(0, 6 << 20),
        [pltpu.VMEM((rows, plan.size, plan.cols), F32)],
    )


def send_far(plan, pieces):
    if plan.shifts is None:
        return [swapped(pieces[0], "mesh")]
    return [shifted(piece, "mesh", d) for d, piece in zip(plan.shifts, pieces)]


def per_device(kern_blocks, kern_cols, state_kernel, start_v, mu, nu):
    plan = Plan(kern_blocks, start_v)
    me, mine = lax.axis_index("mesh"), lax.axis_index("state")
    where = jnp.stack([mine, me]).astype(jnp.int32)
    left_index = (me + plan.peers - 1) % plan.peers
    right_index = (me + 1) % plan.peers
    flat_cols = kern_cols.reshape(-1)
    owners = flat_cols // plan.rows
    places = flat_cols % plan.rows
    near_source = jnp.where(
        owners == left_index,
        places - (plan.rows - plan.near),
        jnp.where(owners == right_index, plan.near + plan.rows + places, plan.near + places),
    )
    remote = (owners != me) & (owners != left_index) & (owners != right_index)
    ref_slots, requests = request_plan(owners, places, remote, plan.peers, plan.rows, CAP_FAR)
    asked = swapped(requests, "mesh").reshape(-1)
    sources = jnp.where(remote, plan.far_base + owners * CAP_FAR + ref_slots, near_source)

    own = start_v.astype(BF16).reshape(plan.rows, plan.size, plan.cols)
    nu = nu.reshape(plan.rows, plan.size, plan.cols)
    head, tail = own[: plan.near], own[plan.rows - plan.near :]
    far = first_far(plan, where, asked, own)
    kern, state_kernel, nu, mu = here(kern_blocks), here(state_kernel), here(nu), here(mu)
    potential_u = None
    for sweep in range(ITERS):
        final = sweep == ITERS - 1
        from_left, from_right = shifted(tail, "mesh", 1), shifted(head, "mesh", -1)
        far = send_far(plan, far)
        spread = []
        for c in range(plan.chunks):
            parts = forward_chunk(plan, c, where, sources, kern, own, from_left, from_right, far)
            spread.append(
                [parts[0]] + [shifted(parts[p], "state", -p) for p in range(1, plan.states)]
            )
        returned = []
        for c in range(plan.chunks):
            parts, potential_u = mix_chunk(
                plan, c, where, spread[c], state_kernel, mu, potential_u, final
            )
            returned.append(
                [parts[0]] + [shifted(parts[p], "state", p) for p in range(1, plan.states)]
            )
        total = None
        for c in range(plan.chunks):
            out = backward_chunk(plan, c, where, sources, kern, returned[c], total)
            total = out[-1]
        own_part, to_left, to_right, to_far = out[0], out[1], out[2], out[3:-1]
        from_right, from_left = shifted(to_left, "mesh", -1), shifted(to_right, "mesh", 1)
        arrived = send_far(plan, to_far)
        out = divide(plan, where, asked, own_part, from_right, from_left, arrived, nu, final)
        if final:
            values = out[0]
        else:
            own, head, tail, far = out[0], out[1], out[2], out[3:]
    return (potential_u, values.reshape(start_v.shape))


def solution(mesh):
    placed = (
        P("mesh", None, None, None),
        P("mesh", None),
        P(),
        P("mesh", "state"),
        P(("mesh", "state"), None),
        P("mesh", "state"),
    )
    return jax.shard_map(
        per_device,
        mesh=mesh,
        in_specs=placed,
        out_specs=(P(("mesh", "state"), None), P("mesh", "state")),
        check_vma=False,
    )
```

```python
import functools

import jax
import jax.numpy as jnp
from jax import lax
from jax.experimental import pallas as pl
from jax.experimental.pallas import tpu as pltpu
from jax.sharding import PartitionSpec as P

CAP_FAR = 2
ITERS = 2
CAP_NEAR = 6


VMEM = pl.BlockSpec(memory_space=pltpu.VMEM)
SMEM = pl.BlockSpec(memory_space=pltpu.SMEM)
ANY = pl.BlockSpec(memory_space=pl.ANY)
PARAMS = pltpu.CompilerParams(vmem_limit_bytes=16 << 20)
F32, BF16 = jnp.float32, jnp.bfloat16
MOST_SHIFTS = 8


def here(value):
    return pltpu.with_memory_space_constraint(value, pltpu.VMEM)


def shifted(value, axis, steps):
    count = lax.axis_size(axis)
    return lax.ppermute(value, axis, [(i, (i + steps) % count) for i in range(count)])


def swapped(value, axis):
    return lax.all_to_all(value, axis, split_axis=0, concat_axis=0, tiled=True)


class Plan:
    def __init__(self, kern_blocks, start_v):
        self.rows, self.degree, self.size, _ = kern_blocks.shape
        self.cols = start_v.shape[1]
        self.peers = lax.axis_size("mesh")
        self.states = lax.axis_size("state")
        self.near, self.far = CAP_NEAR, CAP_FAR
        self.far_base = self.rows + 2 * self.near
        self.table = self.far_base + self.peers * self.far
        self.share = self.rows // self.states
        self.shifts = range(2, self.peers - 1) if self.peers <= MOST_SHIFTS else None
        self.order = sorted(range(1, self.states), key=lambda p: abs(2 * p - self.states))

    def blocks(self, count, dtype):
        return pltpu.VMEM((count, self.size, self.cols), dtype)

    def far_blocks(self):
        if self.shifts is None:
            return [self.blocks(self.peers * self.far, BF16)]
        return [self.blocks(self.far, BF16)] * len(self.shifts)

    def far_slots(self, way):
        if self.shifts is None:
            return [(t, 0, t) for t in range(self.peers * self.far)]
        slots = []
        for i, shift in enumerate(self.shifts):
            peer = lax.rem(lax.axis_index("mesh") + way * shift + self.peers, self.peers)
            slots += [(peer * self.far + t, i, t) for t in range(self.far)]
        return slots

    def cost(self, matmul_blocks, nbytes):
        flops = 2 * matmul_blocks * self.size * self.size * self.cols
        return pl.CostEstimate(flops=flops, bytes_accessed=nbytes, transcendentals=0)

    def rows_of(self, p):
        return lax.rem(lax.axis_index("state") - p + self.states, self.states) * self.share


def call(kernel, name, out_shape, in_specs, args, cost, scratch=(), aliases={}, out_specs=None):
    args = [here(a) if spec is VMEM else a for spec, a in zip(in_specs, args)]
    return pl.pallas_call(
        kernel,
        name=name,
        out_shape=out_shape,
        in_specs=in_specs,
        out_specs=[VMEM] * len(out_shape) if out_specs is None else out_specs,
        scratch_shapes=list(scratch),
        input_output_aliases=aliases,
        compiler_params=PARAMS,
        cost_estimate=cost,
    )(*args)


def begin(plan, kern_cols, start_v):
    rows, near, peers, far = plan.rows, plan.near, plan.peers, plan.far
    n_ask = 1 if plan.shifts is None else len(plan.shifts)

    def kernel(cols_ref, v_hbm, src_ref, *rest):
        asks, (own, head, tail, buf, sem) = rest[:n_ask], rest[n_ask:]
        load = pltpu.make_async_copy(v_hbm, buf, sem)
        load.start()
        me = lax.axis_index("mesh")
        cols = cols_ref[...]
        before, after = lax.rem(me + peers - 1, peers), lax.rem(me + 1, peers)
        src = cols - me * rows + near
        src = jnp.where(cols // rows == before, cols - before * rows - (rows - near), src)
        src = jnp.where(cols // rows == after, cols - after * rows + near + rows, src)
        for d in range(peers) if plan.shifts is None else plan.shifts:
            peer = d if plan.shifts is None else lax.rem(me + d, peers)
            place = cols - peer * rows
            of_peer = (place >= 0) & (place < rows)
            if plan.shifts is None:
                of_peer &= (peer != me) & (peer != before) & (peer != after)
            least = jnp.min(jnp.where(of_peer, place, rows))
            most = jnp.max(jnp.where(of_peer, place, 0))
            slot = plan.far_base + peer * far
            src = jnp.where(of_peer, slot + (place != least).astype(jnp.int32), src)
            ask, at = (asks[0], d * far) if plan.shifts is None else (asks[d - 2], 0)
            ask[at] = jnp.minimum(least, most)
            ask[at + 1] = most
        src_ref[...] = src
        load.wait()
        for t in range(rows):
            value = buf[t].astype(BF16)
            own[t] = value
            if t < near:
                head[t] = value
            if t >= rows - near:
                tail[t - rows + near] = value

    ask = jax.ShapeDtypeStruct((peers * far if plan.shifts is None else far,), jnp.int32)
    out = call(
        kernel,
        "begin",
        [pltpu.VMEM(kern_cols.shape, jnp.int32)]
        + [ask] * n_ask
        + [plan.blocks(n, BF16) for n in (rows, near, near)],
        [VMEM, ANY],
        [kern_cols, start_v],
        plan.cost(0, 3 << 20),
        [pltpu.VMEM(start_v.shape, F32), pltpu.SemaphoreType.DMA],
        out_specs=[VMEM] + [SMEM] * n_ask + [VMEM] * 3,
    )
    return out[0], list(out[1 : 1 + n_ask]), out[1 + n_ask :]


def forward(plan, p, sources, kern, inputs, table):
    share, degree, near, rows = plan.share, plan.degree, plan.near, plan.rows
    gathers = table is None
    n_in = len(inputs) if gathers else 1

    def kernel(src, kern_ref, *rest):
        out, tbl = rest[n_in], rest[n_in + 1] if gathers else rest[0]
        if gathers:
            own_ref, left_ref, right_ref = rest[:3]
            far_refs = rest[3:n_in]
            for t in range(near):
                tbl[t] = left_ref[t]
                tbl[near + rows + t] = right_ref[t]
            for t in range(rows):
                tbl[near + t] = own_ref[t]
            for slot, i, t in plan.far_slots(-1):
                tbl[plan.far_base + slot] = far_refs[i][t]
        first = plan.rows_of(p)
        for g in range(share):
            row = first + g
            lhs = jnp.concatenate([kern_ref[row, k] for k in range(degree)], axis=1)
            rhs = jnp.concatenate([tbl[src[row, k]] for k in range(degree)], axis=0)
            out[g] = jnp.dot(lhs, rhs, preferred_element_type=F32).astype(BF16)

    out = call(
        kernel,
        "forward",
        [plan.blocks(share, BF16)] + ([plan.blocks(plan.table, BF16)] if gathers else []),
        [SMEM] + [VMEM] * (1 + n_in),
        [sources, kern] + (list(inputs) if gathers else [table]),
        plan.cost(share * degree, 4 << 20),
    )
    return out[0], out[1] if gathers else table


def turned(plan, k_ref, p):
    at = lax.rem(lax.axis_index("state") + p, plan.states) * plan.cols
    return k_ref[:, pl.ds(pl.multiple_of(at, plan.cols), plan.cols)]


def mix(plan, pieces, state_kernel, mu, p_first, final):
    states, share, size, cols = plan.states, plan.share, plan.size, plan.cols

    def kernel(*refs):
        a_refs, (k_ref, mu_ref), rest = refs[:states], refs[states : states + 2], refs[states + 2 :]
        rounded, out = rest[:2]
        k_in = jnp.concatenate([turned(plan, k_ref, p) for p in range(states)], axis=1)
        k_out = turned(plan, k_ref, p_first)
        copies = []
        for g in range(share):
            a = jnp.concatenate([ref[g] for ref in a_refs], axis=1)
            mixed = lax.dot_general(a, k_in, (((1,), (1,)), ((), ())), preferred_element_type=F32)
            u = mu_ref[pl.ds(g * size, size), :] / mixed
            if final:
                u_ref, u_buf, sem = rest[2:]
                u_buf[g] = u
                copy = pltpu.make_async_copy(
                    u_buf.at[g], u_ref.at[pl.ds(g * size, size), :], sem.at[g]
                )
                copy.start()
                copies.append(copy)
            u = u.astype(BF16)
            rounded[g] = u
            out[g] = jnp.dot(u, k_out, preferred_element_type=F32).astype(BF16)
        for copy in copies:
            copy.wait()

    width = mu.shape[1]
    out_shape = [pltpu.VMEM((share, size, width), BF16), plan.blocks(share, BF16)]
    out_specs, scratch = [VMEM] * 2, []
    if final:
        out_shape.append(jax.ShapeDtypeStruct(mu.shape, F32))
        out_specs.append(ANY)
        scratch = [pltpu.VMEM((share, size, width), F32), pltpu.SemaphoreType.DMA((share,))]
    return call(
        kernel,
        "mix",
        out_shape,
        [VMEM] * (states + 2),
        [*pieces, state_kernel, mu],
        plan.cost(share * states * (states + 1), 4 << 20),
        scratch,
        out_specs=out_specs,
    )


def mix_back(plan, p, rounded, state_kernel):
    def kernel(u_ref, k_ref, out):
        k_out = turned(plan, k_ref, p)
        for g in range(plan.share):
            out[g] = jnp.dot(u_ref[g], k_out, preferred_element_type=F32).astype(BF16)

    return call(
        kernel,
        "mix_back",
        [plan.blocks(plan.share, BF16)],
        [VMEM] * 2,
        [rounded, state_kernel],
        plan.cost(plan.share * plan.states, 1 << 20),
    )[0]


def backward(plan, p, sources, kern, piece, so_far, last):
    share, degree, near, rows = plan.share, plan.degree, plan.near, plan.rows
    n_acc = 0 if so_far is None else 1

    def kernel(src, kern_ref, b_ref, *rest):
        rest = rest[n_acc:]
        acc = rest[-1]
        if not n_acc:
            acc[...] = jnp.zeros_like(acc)
        first = plan.rows_of(p)
        for g in range(share):
            row = first + g
            b = b_ref[g]
            for k in range(degree):
                part = lax.dot_general(
                    kern_ref[row, k], b, (((0,), (0,)), ((), ())), preferred_element_type=F32
                )
                acc[src[row, k]] += part
        if not last:
            return
        own, left, right, far = rest[0], rest[1], rest[2], rest[3:-1]
        for t in range(near):
            left[t] = acc[t].astype(BF16)
            right[t] = acc[near + rows + t].astype(BF16)
        for slot, i, t in plan.far_slots(1):
            far[i][t] = acc[plan.far_base + slot].astype(BF16)
        for t in range(rows):
            own[t] = acc[near + t].astype(BF16)

    out_shape = []
    if last:
        out_shape = [plan.blocks(n, BF16) for n in (rows, near, near)] + plan.far_blocks()
    return call(
        kernel,
        "backward",
        out_shape + [plan.blocks(plan.table, F32)],
        [SMEM] + [VMEM] * (2 + n_acc),
        [sources, kern, piece] + ([] if so_far is None else [so_far]),
        plan.cost(share * degree, 5 << 20),
        (),
        {3: len(out_shape)} if n_acc else {},
    )


def first_far(plan, asked, own):
    def kernel(own_ref, *rest):
        asked_refs, outs = rest[: len(asked)], rest[len(asked) :]
        for _, i, t in plan.far_slots(1):
            outs[i][t] = own_ref[asked_refs[i][t]]

    return call(
        kernel,
        "first_far",
        plan.far_blocks(),
        [VMEM] + [SMEM] * len(asked),
        [own, *asked],
        plan.cost(0, 2 << 20),
    )


def divide(plan, asked, own, from_right, from_left, arrived, nu, final):
    near, rows, n_far = plan.near, plan.rows, len(arrived)

    def kernel(own_ref, right_ref, left_ref, nu_ref, *rest):
        far_refs, asked_refs, outs, acc = (
            rest[:n_far],
            rest[n_far : 2 * n_far],
            rest[2 * n_far : -1],
            rest[-1],
        )
        for t in range(rows):
            value = own_ref[t].astype(F32)
            if t < near:
                value = value + left_ref[t].astype(F32)
            if t >= rows - near:
                value = value + right_ref[t - rows + near].astype(F32)
            acc[t] = value
        for _, i, t in plan.far_slots(-1):
            acc[asked_refs[n_far - 1 - i][t]] += far_refs[i][t].astype(F32)
        for t in range(rows):
            value = nu_ref[t] / acc[t]
            if final:
                outs[0][t] = value
            else:
                value = value.astype(BF16)
                outs[0][t] = value
                if t < near:
                    outs[1][t] = value
                if t >= rows - near:
                    outs[2][t - rows + near] = value
        if not final:
            for _, i, t in plan.far_slots(1):
                outs[3 + i][t] = outs[0][asked_refs[i][t]]

    if final:
        out_shape = [jax.ShapeDtypeStruct((rows, plan.size, plan.cols), F32)]
    else:
        out_shape = [plan.blocks(n, BF16) for n in (rows, near, near)] + plan.far_blocks()
    return call(
        kernel,
        "divide",
        out_shape,
        [VMEM] * (4 + n_far) + [SMEM] * n_far,
        [own, from_right, from_left, nu, *arrived, *asked],
        plan.cost(0, 6 << 20),
        [pltpu.VMEM((rows, plan.size, plan.cols), F32)],
    )


def send_far(plan, pieces):
    if plan.shifts is None:
        return [swapped(pieces[0], "mesh")]
    return [shifted(piece, "mesh", d) for d, piece in zip(plan.shifts, pieces)]


def send_asks(plan, asks):
    if plan.shifts is None:
        pairs = asks[0].reshape(plan.peers, plan.far)
        return [swapped(pairs, "mesh").reshape(-1)]
    return send_far(plan, asks)[::-1]


def per_device(kern_blocks, kern_cols, state_kernel, start_v, mu, nu):
    plan = Plan(kern_blocks, start_v)
    shape = (plan.rows, plan.size, plan.cols)
    sources, asks, (own, head, tail) = begin(plan, kern_cols, start_v.reshape(shape))
    asked = send_asks(plan, asks)
    far = first_far(plan, asked, own)
    nu = nu.reshape(shape)
    kern, state_kernel, nu, mu = here(kern_blocks), here(state_kernel), here(nu), here(mu)
    for sweep in range(ITERS):
        final = sweep == ITERS - 1
        from_left, from_right = shifted(tail, "mesh", 1), shifted(head, "mesh", -1)
        far = send_far(plan, far)
        inputs, table = [own, from_left, from_right, *far], None
        pieces = [None] * plan.states
        for p in [*plan.order, 0]:
            part, table = forward(plan, p, sources, kern, inputs, table)
            pieces[p] = shifted(part, "state", -p) if p else part
        out = mix(plan, pieces, state_kernel, mu, plan.order[0], final)
        rounded, part = out[0], out[1]
        if final:
            potential_u = out[2]
        pieces = [None] * plan.states
        for p in [*plan.order, 0]:
            if p != plan.order[0]:
                part = mix_back(plan, p, rounded, state_kernel)
            pieces[p] = shifted(part, "state", p) if p else part
        total = None
        for p in [0, *plan.order]:
            out = backward(
                plan, p, sources, kern, pieces[p], total, p == plan.order[-1]
            )
            total = out[-1]
        own_part, to_left, to_right, to_far = out[0], out[1], out[2], out[3:-1]
        from_right, from_left = shifted(to_left, "mesh", -1), shifted(to_right, "mesh", 1)
        arrived = send_far(plan, to_far)
        out = divide(plan, asked, own_part, from_right, from_left, arrived, nu, final)
        if final:
            values = out[0]
        else:
            own, head, tail, far = out[0], out[1], out[2], out[3:]
    return (potential_u, values.reshape(start_v.shape))


def solution(mesh):
    placed = (
        P("mesh", None, None, None),
        P("mesh", None),
        P(),
        P("mesh", "state"),
        P(("mesh", "state"), None),
        P("mesh", "state"),
    )
    return jax.shard_map(
        per_device,
        mesh=mesh,
        in_specs=placed,
        out_specs=(P(("mesh", "state"), None), P("mesh", "state")),
        check_vma=False,
    )
```

```python
import jax
import jax.numpy as jnp
from jax import lax
from jax.experimental import pallas as pl
from jax.experimental.pallas import tpu as pltpu
from jax.sharding import PartitionSpec as P

CAP_FAR = 2
ITERS = 2
CAP_NEAR = 6


VMEM = pl.BlockSpec(memory_space=pltpu.VMEM)
SMEM = pl.BlockSpec(memory_space=pltpu.SMEM)
INDEX = pl.BlockSpec(memory_space=pltpu.SMEM)
ANY = pl.BlockSpec(memory_space=pl.ANY)
PARAMS = pltpu.CompilerParams(vmem_limit_bytes=16 << 20)
F32, BF16 = jnp.float32, jnp.bfloat16
MOST_SHIFTS = 8


def in_smem(value):
    return pltpu.with_memory_space_constraint(value, pltpu.SMEM)


def here(value):
    return pltpu.with_memory_space_constraint(value, pltpu.VMEM)


def shifted(value, axis, steps):
    count = lax.axis_size(axis)
    return lax.ppermute(value, axis, [(i, (i + steps) % count) for i in range(count)])


def swapped(value, axis):
    return lax.all_to_all(value, axis, split_axis=0, concat_axis=0, tiled=True)


class Plan:
    def __init__(self, kern_blocks, start_v):
        self.rows, self.degree, self.size, _ = kern_blocks.shape
        self.cols = start_v.shape[1]
        self.peers = lax.axis_size("mesh")
        self.states = lax.axis_size("state")
        self.near, self.far = CAP_NEAR, CAP_FAR
        self.far_base = self.rows + 2 * self.near
        self.table = self.far_base + self.peers * self.far
        self.share = self.rows // self.states
        self.shifts = range(2, self.peers - 1) if self.peers <= MOST_SHIFTS else None
        self.order = sorted(range(1, self.states), key=lambda p: abs(2 * p - self.states))

    def blocks(self, count, dtype):
        return pltpu.VMEM((count, self.size, self.cols), dtype)

    def far_blocks(self):
        if self.shifts is None:
            return [self.blocks(self.peers * self.far, BF16)]
        return [self.blocks(self.far, BF16)] * len(self.shifts)

    def far_slots(self, way):
        if self.shifts is None:
            return [(t, 0, t) for t in range(self.peers * self.far)]
        slots = []
        for i, shift in enumerate(self.shifts):
            peer = lax.rem(lax.axis_index("mesh") + way * shift + self.peers, self.peers)
            slots += [(peer * self.far + t, i, t) for t in range(self.far)]
        return slots

    def cost(self, matmul_blocks, nbytes):
        flops = 2 * matmul_blocks * self.size * self.size * self.cols
        return pl.CostEstimate(flops=flops, bytes_accessed=nbytes, transcendentals=0)

    def rows_of(self, p):
        return lax.rem(lax.axis_index("state") - p + self.states, self.states) * self.share


def call(kernel, out_shape, in_specs, args, cost, scratch=(), aliases={}, out_specs=None):
    args = [here(a) if spec is VMEM else a for spec, a in zip(in_specs, args)]
    args = [in_smem(a) if spec is INDEX else a for spec, a in zip(in_specs, args)]
    return pl.pallas_call(
        kernel,
        out_shape=out_shape,
        in_specs=in_specs,
        out_specs=[VMEM] * len(out_shape) if out_specs is None else out_specs,
        scratch_shapes=list(scratch),
        input_output_aliases=aliases,
        compiler_params=PARAMS,
        cost_estimate=cost,
    )(*args)


def begin(plan, kern_cols, start_v):
    rows, near, peers, far = plan.rows, plan.near, plan.peers, plan.far
    n_ask = 1 if plan.shifts is None else len(plan.shifts)

    def kernel(cols_ref, v_hbm, src_ref, *rest):
        asks, (own, head, tail, buf, src_buf, sem) = rest[:n_ask], rest[n_ask:]
        load = pltpu.make_async_copy(v_hbm, buf, sem)
        load.start()
        me = lax.axis_index("mesh")
        cols = cols_ref[...]
        before, after = lax.rem(me + peers - 1, peers), lax.rem(me + 1, peers)
        src = cols - me * rows + near
        src = jnp.where(cols // rows == before, cols - before * rows - (rows - near), src)
        src = jnp.where(cols // rows == after, cols - after * rows + near + rows, src)
        for d in range(peers) if plan.shifts is None else plan.shifts:
            peer = d if plan.shifts is None else lax.rem(me + d, peers)
            place = cols - peer * rows
            of_peer = (place >= 0) & (place < rows)
            if plan.shifts is None:
                of_peer &= (peer != me) & (peer != before) & (peer != after)
            least = jnp.min(jnp.where(of_peer, place, rows))
            most = jnp.max(jnp.where(of_peer, place, 0))
            slot = plan.far_base + peer * far
            src = jnp.where(of_peer, slot + (place != least).astype(jnp.int32), src)
            ask, at = (asks[0], d * far) if plan.shifts is None else (asks[d - 2], 0)
            ask[at] = jnp.minimum(least, most)
            ask[at + 1] = most
        src_buf[...] = src
        load.wait()
        index = pltpu.make_async_copy(src_buf, src_ref, sem)
        index.start()
        for t in range(rows):
            value = buf[t].astype(BF16)
            own[t] = value
            if t < near:
                head[t] = value
            if t >= rows - near:
                tail[t - rows + near] = value
        index.wait()

    ask = jax.ShapeDtypeStruct((peers * far if plan.shifts is None else far,), jnp.int32)
    out = call(
        kernel,
        [pltpu.SMEM(kern_cols.shape, jnp.int32)]
        + [ask] * n_ask
        + [plan.blocks(n, BF16) for n in (rows, near, near)],
        [VMEM, ANY],
        [kern_cols, start_v],
        plan.cost(0, 3 << 20),
        [
            pltpu.VMEM(start_v.shape, F32),
            pltpu.VMEM(kern_cols.shape, jnp.int32),
            pltpu.SemaphoreType.DMA,
        ],
        out_specs=[INDEX] + [SMEM] * n_ask + [VMEM] * 3,
    )
    return out[0], list(out[1 : 1 + n_ask]), out[1 + n_ask :]


def forward(plan, p, sources, kern, inputs, table, first_time):
    share, degree, near, rows = plan.share, plan.degree, plan.near, plan.rows
    gathers = table is None
    n_in = len(inputs) if gathers else 1

    def kernel(src, kern_ref, *rest):
        ins, outs = rest[:n_in], rest[n_in:]
        out, tbl = outs[0], outs[1] if gathers else ins[0]
        first = plan.rows_of(p)
        held = kern_ref
        if first_time:
            held, sem = outs[-2:]
            loads = [
                pltpu.make_async_copy(kern_ref.at[first + g], held.at[g], sem.at[g])
                for g in range(share)
            ]
            for load in loads:
                load.start()
        if gathers:
            own_ref, left_ref, right_ref = ins[:3]
            far_refs = ins[3:]
            for t in range(near):
                tbl[t] = left_ref[t]
                tbl[near + rows + t] = right_ref[t]
            for t in range(rows):
                tbl[near + t] = own_ref[t]
            for slot, i, t in plan.far_slots(-1):
                tbl[plan.far_base + slot] = far_refs[i][t]
        for g in range(share):
            if first_time:
                loads[g].wait()
            row = first + g
            lhs = jnp.concatenate([held[g, k] for k in range(degree)], axis=1)
            rhs = jnp.concatenate([tbl[src[row, k]] for k in range(degree)], axis=0)
            out[g] = jnp.dot(lhs, rhs, preferred_element_type=F32).astype(BF16)

    out_shape = [plan.blocks(share, BF16)]
    if gathers:
        out_shape.append(plan.blocks(plan.table, BF16))
    if first_time:
        out_shape.append(pltpu.VMEM((share, *kern.shape[1:]), BF16))
    out = call(
        kernel,
        out_shape,
        [INDEX, ANY if first_time else VMEM] + [VMEM] * n_in,
        [sources, kern] + (list(inputs) if gathers else [table]),
        plan.cost(share * degree, 4 << 20),
        [pltpu.SemaphoreType.DMA((share,))] if first_time else (),
    )
    return out[0], out[1] if gathers else table, out[-1] if first_time else kern


def turned(plan, k_ref, p):
    at = lax.rem(lax.axis_index("state") + p, plan.states) * plan.cols
    return k_ref[:, pl.ds(pl.multiple_of(at, plan.cols), plan.cols)]


def mix(plan, pieces, state_kernel, mu, p_first, final):
    states, share, size = plan.states, plan.share, plan.size

    def kernel(*refs):
        a_refs, (k_ref, mu_ref), rest = refs[:states], refs[states : states + 2], refs[states + 2 :]
        rounded, out = rest[:2]
        k_in = jnp.concatenate([turned(plan, k_ref, p) for p in range(states)], axis=1)
        k_out = turned(plan, k_ref, p_first)
        copies = []
        for g in range(share):
            a = jnp.concatenate([ref[g] for ref in a_refs], axis=1)
            mixed = lax.dot_general(a, k_in, (((1,), (1,)), ((), ())), preferred_element_type=F32)
            u = mu_ref[pl.ds(g * size, size), :] / mixed
            if final:
                u_ref, u_buf, sem = rest[2:]
                u_buf[g] = u
                copy = pltpu.make_async_copy(
                    u_buf.at[g], u_ref.at[pl.ds(g * size, size), :], sem.at[g]
                )
                copy.start()
                copies.append(copy)
            u = u.astype(BF16)
            rounded[g] = u
            out[g] = jnp.dot(u, k_out, preferred_element_type=F32).astype(BF16)
        for copy in copies:
            copy.wait()

    width = mu.shape[1]
    out_shape = [pltpu.VMEM((share, size, width), BF16), plan.blocks(share, BF16)]
    out_specs, scratch = [VMEM] * 2, []
    if final:
        out_shape.append(jax.ShapeDtypeStruct(mu.shape, F32))
        out_specs.append(ANY)
        scratch = [pltpu.VMEM((share, size, width), F32), pltpu.SemaphoreType.DMA((share,))]
    return call(
        kernel,
        out_shape,
        [VMEM] * (states + 2),
        [*pieces, state_kernel, mu],
        plan.cost(share * states * (states + 1), 4 << 20),
        scratch,
        out_specs=out_specs,
    )


def mix_back(plan, p, rounded, state_kernel):
    def kernel(u_ref, k_ref, out):
        k_out = turned(plan, k_ref, p)
        for g in range(plan.share):
            out[g] = jnp.dot(u_ref[g], k_out, preferred_element_type=F32).astype(BF16)

    return call(
        kernel,
        [plan.blocks(plan.share, BF16)],
        [VMEM] * 2,
        [rounded, state_kernel],
        plan.cost(plan.share * plan.states, 1 << 20),
    )[0]


def backward(plan, p, sources, kern, piece, so_far, last):
    share, degree, near, rows = plan.share, plan.degree, plan.near, plan.rows
    n_acc = 0 if so_far is None else 1

    def kernel(src, kern_ref, b_ref, *rest):
        rest = rest[n_acc:]
        acc = rest[-1]
        if not n_acc:
            acc[...] = jnp.zeros_like(acc)
        first = plan.rows_of(p)
        for g in range(share):
            row = first + g
            b = b_ref[g]
            for k in range(degree):
                part = lax.dot_general(
                    kern_ref[g, k], b, (((0,), (0,)), ((), ())), preferred_element_type=F32
                )
                acc[src[row, k]] += part
        if not last:
            return
        own, left, right, far = rest[0], rest[1], rest[2], rest[3:-1]
        for t in range(near):
            left[t] = acc[t].astype(BF16)
            right[t] = acc[near + rows + t].astype(BF16)
        for slot, i, t in plan.far_slots(1):
            far[i][t] = acc[plan.far_base + slot].astype(BF16)
        for t in range(rows):
            own[t] = acc[near + t].astype(BF16)

    out_shape = []
    if last:
        out_shape = [plan.blocks(n, BF16) for n in (rows, near, near)] + plan.far_blocks()
    return call(
        kernel,
        out_shape + [plan.blocks(plan.table, F32)],
        [INDEX] + [VMEM] * (2 + n_acc),
        [sources, kern, piece] + ([] if so_far is None else [so_far]),
        plan.cost(share * degree, 5 << 20),
        (),
        {3: len(out_shape)} if n_acc else {},
    )


def first_far(plan, asked, own):
    def kernel(own_ref, *rest):
        asked_refs, outs = rest[: len(asked)], rest[len(asked) :]
        for _, i, t in plan.far_slots(1):
            outs[i][t] = own_ref[asked_refs[i][t]]

    return call(
        kernel,
        plan.far_blocks(),
        [VMEM] + [SMEM] * len(asked),
        [own, *asked],
        plan.cost(0, 2 << 20),
    )


def divide(plan, asked, own, from_right, from_left, arrived, nu, final):
    near, rows, n_far = plan.near, plan.rows, len(arrived)

    def kernel(own_ref, right_ref, left_ref, nu_ref, *rest):
        far_refs, asked_refs, outs, acc = (
            rest[:n_far],
            rest[n_far : 2 * n_far],
            rest[2 * n_far : -1],
            rest[-1],
        )
        for t in range(rows):
            value = own_ref[t].astype(F32)
            if t < near:
                value = value + left_ref[t].astype(F32)
            if t >= rows - near:
                value = value + right_ref[t - rows + near].astype(F32)
            acc[t] = value
        for _, i, t in plan.far_slots(-1):
            acc[asked_refs[n_far - 1 - i][t]] += far_refs[i][t].astype(F32)
        for t in range(rows):
            value = nu_ref[t] / acc[t]
            if final:
                outs[0][t] = value
            else:
                value = value.astype(BF16)
                outs[0][t] = value
                if t < near:
                    outs[1][t] = value
                if t >= rows - near:
                    outs[2][t - rows + near] = value
        if not final:
            for _, i, t in plan.far_slots(1):
                outs[3 + i][t] = outs[0][asked_refs[i][t]]

    if final:
        out_shape = [jax.ShapeDtypeStruct((rows, plan.size, plan.cols), F32)]
    else:
        out_shape = [plan.blocks(n, BF16) for n in (rows, near, near)] + plan.far_blocks()
    return call(
        kernel,
        out_shape,
        [VMEM] * (4 + n_far) + [SMEM] * n_far,
        [own, from_right, from_left, nu, *arrived, *asked],
        plan.cost(0, 6 << 20),
        [pltpu.VMEM((rows, plan.size, plan.cols), F32)],
    )


def send_far(plan, pieces):
    if plan.shifts is None:
        return [swapped(pieces[0], "mesh")]
    out = []
    for d, piece in zip(plan.shifts, pieces):
        out.append(shifted(piece, "mesh", d))
    return out


def send_asks(plan, asks):
    if plan.shifts is None:
        pairs = asks[0].reshape(plan.peers, plan.far)
        return [swapped(pairs, "mesh").reshape(-1)]
    return send_far(plan, asks)[::-1]


def send_near(to_left, to_right):
    from_left = shifted(to_right, "mesh", 1)
    from_right = shifted(to_left, "mesh", -1)
    return from_left, from_right


def sweep_once(plan, state, sources, asked, kern, kept, state_kernel, mu, nu, first_time, final):
    own, head, tail, far = state
    from_left, from_right = send_near(head, tail)
    far = send_far(plan, far)
    inputs, table = [own, from_left, from_right, *far], None
    pieces = [None] * plan.states
    for p in [*plan.order, 0]:
        part, table, kept[p] = forward(
            plan, p, sources, kern if first_time else kept[p], inputs, table, first_time
        )
        pieces[p] = shifted(part, "state", -p) if p else part
    out = mix(plan, pieces, state_kernel, mu, plan.order[0], final)
    rounded, part, potential_u = out[0], out[1], out[-1]
    pieces = [None] * plan.states
    for p in [*plan.order, 0]:
        if p != plan.order[0]:
            part = mix_back(plan, p, rounded, state_kernel)
        pieces[p] = shifted(part, "state", p) if p else part
    total = None
    for p in [0, *plan.order]:
        out = backward(
            plan, p, sources, kept[p], pieces[p], total, p == plan.order[-1]
        )
        total = out[-1]
    own_part, to_left, to_right, to_far = out[0], out[1], out[2], out[3:-1]
    from_left, from_right = send_near(to_left, to_right)
    arrived = send_far(plan, to_far)
    out = divide(plan, asked, own_part, from_right, from_left, arrived, nu, final)
    return potential_u, out


def per_device(kern_blocks, kern_cols, state_kernel, start_v, mu, nu):
    plan = Plan(kern_blocks, start_v)
    shape = (plan.rows, plan.size, plan.cols)
    nu = nu.reshape(shape)
    kept = [None] * plan.states
    for sweep in range(ITERS):
        if sweep == 0:
            sources, asks, (own, head, tail) = begin(plan, kern_cols, start_v.reshape(shape))
            asked = send_asks(plan, asks)
            state = (own, head, tail, first_far(plan, asked, own))
        potential_u, out = sweep_once(
            plan,
            state,
            sources,
            asked,
            kern_blocks,
            kept,
            state_kernel,
            mu,
            nu,
            sweep == 0,
            sweep == ITERS - 1,
        )
        state = (out[0], *out[1:3], out[3:])
    return (potential_u, out[0].reshape(start_v.shape))


def solution(mesh):
    placed = (
        P("mesh", None, None, None),
        P("mesh", None),
        P(),
        P("mesh", "state"),
        P(("mesh", "state"), None),
        P("mesh", "state"),
    )
    return jax.shard_map(
        per_device,
        mesh=mesh,
        in_specs=placed,
        out_specs=(P(("mesh", "state"), None), P("mesh", "state")),
        check_vma=False,
    )
```

```python
import jax
import jax.numpy as jnp
from jax import lax
from jax.experimental import pallas as pl
from jax.experimental.pallas import tpu as pltpu
from jax.sharding import PartitionSpec as P

CAP_FAR = 2
ITERS = 2
CAP_NEAR = 6


VMEM = pl.BlockSpec(memory_space=pltpu.VMEM)
SMEM = pl.BlockSpec(memory_space=pltpu.SMEM)
INDEX = pl.BlockSpec(memory_space=pltpu.SMEM)
ANY = pl.BlockSpec(memory_space=pl.ANY)
HBM = pl.BlockSpec(memory_space=pltpu.HBM)
PARAMS = pltpu.CompilerParams(vmem_limit_bytes=16 << 20)
F32, BF16 = jnp.float32, jnp.bfloat16
MOST_SHIFTS = 8


def in_smem(value):
    return pltpu.with_memory_space_constraint(value, pltpu.SMEM)


def in_hbm(value):
    return pltpu.with_memory_space_constraint(value, pltpu.HBM)


def here(value):
    return pltpu.with_memory_space_constraint(value, pltpu.VMEM)


def shifted(value, axis, steps):
    count = lax.axis_size(axis)
    return lax.ppermute(value, axis, [(i, (i + steps) % count) for i in range(count)])


def swapped(value, axis):
    return lax.all_to_all(value, axis, split_axis=0, concat_axis=0, tiled=True)


class Plan:
    def __init__(self, kern_blocks, start_v):
        self.rows, self.degree, self.size, _ = kern_blocks.shape
        self.cols = start_v.shape[1]
        self.peers = lax.axis_size("mesh")
        self.states = lax.axis_size("state")
        self.near, self.far = CAP_NEAR, CAP_FAR
        self.far_base = self.rows + 2 * self.near
        self.table = self.far_base + self.peers * self.far
        self.share = self.rows // self.states
        self.shifts = range(2, self.peers - 1) if self.peers <= MOST_SHIFTS else None
        self.order = sorted(range(1, self.states), key=lambda p: abs(2 * p - self.states))

    def blocks(self, count, dtype):
        return pltpu.VMEM((count, self.size, self.cols), dtype)

    def far_blocks(self):
        if self.shifts is None:
            return [self.blocks(self.peers * self.far, BF16)]
        return [self.blocks(self.far, BF16)] * len(self.shifts)

    def far_slots(self, way):
        if self.shifts is None:
            return [(t, 0, t) for t in range(self.peers * self.far)]
        slots = []
        for i, shift in enumerate(self.shifts):
            peer = lax.rem(lax.axis_index("mesh") + way * shift + self.peers, self.peers)
            slots += [(peer * self.far + t, i, t) for t in range(self.far)]
        return slots

    def cost(self, matmul_blocks, nbytes):
        flops = 2 * matmul_blocks * self.size * self.size * self.cols
        return pl.CostEstimate(flops=flops, bytes_accessed=nbytes, transcendentals=0)

    def rows_of(self, p):
        return lax.rem(lax.axis_index("state") - p + self.states, self.states) * self.share


def call(kernel, out_shape, in_specs, args, cost, scratch=(), aliases={}, out_specs=None):
    args = [here(a) if spec is VMEM else a for spec, a in zip(in_specs, args)]
    args = [in_smem(a) if spec is INDEX else a for spec, a in zip(in_specs, args)]
    args = [in_hbm(a) if spec is HBM else a for spec, a in zip(in_specs, args)]
    return pl.pallas_call(
        kernel,
        out_shape=out_shape,
        in_specs=in_specs,
        out_specs=[VMEM] * len(out_shape) if out_specs is None else out_specs,
        scratch_shapes=list(scratch),
        input_output_aliases=aliases,
        compiler_params=PARAMS,
        cost_estimate=cost,
    )(*args)


def begin(plan, kern_cols, start_v):
    rows, near, peers, far = plan.rows, plan.near, plan.peers, plan.far
    n_ask = 1 if plan.shifts is None else len(plan.shifts)

    def kernel(cols_ref, v_hbm, src_ref, *rest):
        asks, (own, head, tail, buf, src_buf, sem) = rest[:n_ask], rest[n_ask:]
        load = pltpu.make_async_copy(v_hbm, buf, sem)
        load.start()
        me = lax.axis_index("mesh")
        cols = cols_ref[...]
        before, after = lax.rem(me + peers - 1, peers), lax.rem(me + 1, peers)
        src = cols - me * rows + near
        src = jnp.where(cols // rows == before, cols - before * rows - (rows - near), src)
        src = jnp.where(cols // rows == after, cols - after * rows + near + rows, src)
        for d in range(peers) if plan.shifts is None else plan.shifts:
            peer = d if plan.shifts is None else lax.rem(me + d, peers)
            place = cols - peer * rows
            of_peer = (place >= 0) & (place < rows)
            if plan.shifts is None:
                of_peer &= (peer != me) & (peer != before) & (peer != after)
            least = jnp.min(jnp.where(of_peer, place, rows))
            most = jnp.max(jnp.where(of_peer, place, 0))
            slot = plan.far_base + peer * far
            src = jnp.where(of_peer, slot + (place != least).astype(jnp.int32), src)
            ask, at = (asks[0], d * far) if plan.shifts is None else (asks[d - 2], 0)
            ask[at] = jnp.minimum(least, most)
            ask[at + 1] = most
        src_buf[...] = src
        load.wait()
        index = pltpu.make_async_copy(src_buf, src_ref, sem)
        index.start()
        for t in range(rows):
            value = buf[t].astype(BF16)
            own[t] = value
            if t < near:
                head[t] = value
            if t >= rows - near:
                tail[t - rows + near] = value
        index.wait()

    ask = jax.ShapeDtypeStruct((peers * far if plan.shifts is None else far,), jnp.int32)
    out = call(
        kernel,
        [pltpu.SMEM(kern_cols.shape, jnp.int32)]
        + [ask] * n_ask
        + [plan.blocks(n, BF16) for n in (rows, near, near)],
        [VMEM, HBM],
        [kern_cols, start_v],
        plan.cost(0, 3 << 20),
        [
            pltpu.VMEM(start_v.shape, F32),
            pltpu.VMEM(kern_cols.shape, jnp.int32),
            pltpu.SemaphoreType.DMA,
        ],
        out_specs=[INDEX] + [SMEM] * n_ask + [VMEM] * 3,
    )
    return out[0], list(out[1 : 1 + n_ask]), out[1 + n_ask :]


def forward(plan, p, sources, kern, inputs, table, first_time):
    share, degree, near, rows = plan.share, plan.degree, plan.near, plan.rows
    gathers = table is None
    n_in = len(inputs) if gathers else 1

    def kernel(src, kern_ref, *rest):
        ins, outs = rest[:n_in], rest[n_in:]
        out, tbl = outs[0], outs[1] if gathers else ins[0]
        first = plan.rows_of(p)
        held = kern_ref
        if first_time:
            held, sem = outs[-2:]
            loads = [
                pltpu.make_async_copy(kern_ref.at[first + g], held.at[g], sem.at[g])
                for g in range(share)
            ]
            for load in loads:
                load.start()
        if gathers:
            own_ref, left_ref, right_ref = ins[:3]
            far_refs = ins[3:]
            for t in range(near):
                tbl[t] = left_ref[t]
                tbl[near + rows + t] = right_ref[t]
            for t in range(rows):
                tbl[near + t] = own_ref[t]
            for slot, i, t in plan.far_slots(-1):
                tbl[plan.far_base + slot] = far_refs[i][t]
        for g in range(share):
            if first_time:
                loads[g].wait()
            row = first + g
            lhs = jnp.concatenate([held[g, k] for k in range(degree)], axis=1)
            rhs = jnp.concatenate([tbl[src[row, k]] for k in range(degree)], axis=0)
            out[g] = jnp.dot(lhs, rhs, preferred_element_type=F32).astype(BF16)

    out_shape = [plan.blocks(share, BF16)]
    if gathers:
        out_shape.append(plan.blocks(plan.table, BF16))
    if first_time:
        out_shape.append(pltpu.VMEM((share, *kern.shape[1:]), BF16))
    out = call(
        kernel,
        out_shape,
        [INDEX, HBM if first_time else VMEM] + [VMEM] * n_in,
        [sources, kern] + (list(inputs) if gathers else [table]),
        plan.cost(share * degree, 4 << 20),
        [pltpu.SemaphoreType.DMA((share,))] if first_time else (),
    )
    return out[0], out[1] if gathers else table, out[-1] if first_time else kern


def turned(plan, k_ref, p):
    at = lax.rem(lax.axis_index("state") + p, plan.states) * plan.cols
    return k_ref[:, pl.ds(pl.multiple_of(at, plan.cols), plan.cols)]


def mix(plan, pieces, state_kernel, mu, p_first, final):
    states, share, size = plan.states, plan.share, plan.size

    def kernel(*refs):
        a_refs, (k_ref, mu_ref), rest = refs[:states], refs[states : states + 2], refs[states + 2 :]
        rounded, out = rest[:2]
        k_in = jnp.concatenate([turned(plan, k_ref, p) for p in range(states)], axis=1)
        k_out = turned(plan, k_ref, p_first)
        copies = []
        for g in range(share):
            a = jnp.concatenate([ref[g] for ref in a_refs], axis=1)
            mixed = lax.dot_general(a, k_in, (((1,), (1,)), ((), ())), preferred_element_type=F32)
            u = mu_ref[pl.ds(g * size, size), :] / mixed
            if final:
                u_ref, u_buf, sem = rest[2:]
                u_buf[g] = u
                copy = pltpu.make_async_copy(
                    u_buf.at[g], u_ref.at[pl.ds(g * size, size), :], sem.at[g]
                )
                copy.start()
                copies.append(copy)
            u = u.astype(BF16)
            rounded[g] = u
            out[g] = jnp.dot(u, k_out, preferred_element_type=F32).astype(BF16)
        for copy in copies:
            copy.wait()

    width = mu.shape[1]
    out_shape = [pltpu.VMEM((share, size, width), BF16), plan.blocks(share, BF16)]
    out_specs, scratch = [VMEM] * 2, []
    if final:
        out_shape.append(jax.ShapeDtypeStruct(mu.shape, F32))
        out_specs.append(ANY)
        scratch = [pltpu.VMEM((share, size, width), F32), pltpu.SemaphoreType.DMA((share,))]
    return call(
        kernel,
        out_shape,
        [VMEM] * (states + 2),
        [*pieces, state_kernel, mu],
        plan.cost(share * states * (states + 1), 4 << 20),
        scratch,
        out_specs=out_specs,
    )


def mix_back(plan, p, rounded, state_kernel):
    def kernel(u_ref, k_ref, out):
        k_out = turned(plan, k_ref, p)
        for g in range(plan.share):
            out[g] = jnp.dot(u_ref[g], k_out, preferred_element_type=F32).astype(BF16)

    return call(
        kernel,
        [plan.blocks(plan.share, BF16)],
        [VMEM] * 2,
        [rounded, state_kernel],
        plan.cost(plan.share * plan.states, 1 << 20),
    )[0]


def backward(plan, p, sources, kern, piece, so_far, last):
    share, degree, near, rows = plan.share, plan.degree, plan.near, plan.rows
    n_acc = 0 if so_far is None else 1

    def kernel(src, kern_ref, b_ref, *rest):
        rest = rest[n_acc:]
        acc = rest[-1]
        if not n_acc:
            acc[...] = jnp.zeros_like(acc)
        first = plan.rows_of(p)
        for g in range(share):
            row = first + g
            b = b_ref[g]
            for k in range(degree):
                part = lax.dot_general(
                    kern_ref[g, k], b, (((0,), (0,)), ((), ())), preferred_element_type=F32
                )
                acc[src[row, k]] += part
        if not last:
            return
        own, left, right, far = rest[0], rest[1], rest[2], rest[3:-1]
        for t in range(near):
            left[t] = acc[t].astype(BF16)
            right[t] = acc[near + rows + t].astype(BF16)
        for slot, i, t in plan.far_slots(1):
            far[i][t] = acc[plan.far_base + slot].astype(BF16)
        for t in range(rows):
            own[t] = acc[near + t].astype(BF16)

    out_shape = []
    if last:
        out_shape = [plan.blocks(n, BF16) for n in (rows, near, near)] + plan.far_blocks()
    return call(
        kernel,
        out_shape + [plan.blocks(plan.table, F32)],
        [INDEX] + [VMEM] * (2 + n_acc),
        [sources, kern, piece] + ([] if so_far is None else [so_far]),
        plan.cost(share * degree, 5 << 20),
        (),
        {3: len(out_shape)} if n_acc else {},
    )


def first_far(plan, asked, own):
    def kernel(own_ref, *rest):
        asked_refs, outs = rest[: len(asked)], rest[len(asked) :]
        for _, i, t in plan.far_slots(1):
            outs[i][t] = own_ref[asked_refs[i][t]]

    return call(
        kernel,
        plan.far_blocks(),
        [VMEM] + [SMEM] * len(asked),
        [own, *asked],
        plan.cost(0, 2 << 20),
    )


def divide(plan, asked, own, from_right, from_left, arrived, nu, final):
    near, rows, n_far = plan.near, plan.rows, len(arrived)

    def kernel(own_ref, right_ref, left_ref, nu_ref, *rest):
        far_refs, asked_refs, outs, acc = (
            rest[:n_far],
            rest[n_far : 2 * n_far],
            rest[2 * n_far : -1],
            rest[-1],
        )
        for t in range(rows):
            value = own_ref[t].astype(F32)
            if t < near:
                value = value + left_ref[t].astype(F32)
            if t >= rows - near:
                value = value + right_ref[t - rows + near].astype(F32)
            acc[t] = value
        for _, i, t in plan.far_slots(-1):
            acc[asked_refs[n_far - 1 - i][t]] += far_refs[i][t].astype(F32)
        for t in range(rows):
            value = nu_ref[t] / acc[t]
            if final:
                outs[0][t] = value
            else:
                value = value.astype(BF16)
                outs[0][t] = value
                if t < near:
                    outs[1][t] = value
                if t >= rows - near:
                    outs[2][t - rows + near] = value
        if not final:
            for _, i, t in plan.far_slots(1):
                outs[3 + i][t] = outs[0][asked_refs[i][t]]

    if final:
        out_shape = [jax.ShapeDtypeStruct((rows, plan.size, plan.cols), F32)]
    else:
        out_shape = [plan.blocks(n, BF16) for n in (rows, near, near)] + plan.far_blocks()
    return call(
        kernel,
        out_shape,
        [VMEM] * (4 + n_far) + [SMEM] * n_far,
        [own, from_right, from_left, nu, *arrived, *asked],
        plan.cost(0, 6 << 20),
        [pltpu.VMEM((rows, plan.size, plan.cols), F32)],
    )


def send_far(plan, pieces):
    if plan.shifts is None:
        return [swapped(pieces[0], "mesh")]
    out = []
    for d, piece in zip(plan.shifts, pieces):
        out.append(shifted(piece, "mesh", d))
    return out


def send_asks(plan, asks):
    if plan.shifts is None:
        pairs = asks[0].reshape(plan.peers, plan.far)
        return [swapped(pairs, "mesh").reshape(-1)]
    return send_far(plan, asks)[::-1]


def send_near(to_left, to_right):
    from_left = shifted(to_right, "mesh", 1)
    from_right = shifted(to_left, "mesh", -1)
    return from_left, from_right


def sweep_once(plan, state, sources, asked, kern, kept, state_kernel, mu, nu, first_time, final):
    own, head, tail, far = state
    from_left, from_right = send_near(head, tail)
    far = send_far(plan, far)
    inputs, table = [own, from_left, from_right, *far], None
    pieces = [None] * plan.states
    for p in [*plan.order, 0]:
        part, table, kept[p] = forward(
            plan, p, sources, kern if first_time else kept[p], inputs, table, first_time
        )
        pieces[p] = shifted(part, "state", -p) if p else part
    out = mix(plan, pieces, state_kernel, mu, plan.order[0], final)
    rounded, part, potential_u = out[0], out[1], out[-1]
    pieces = [None] * plan.states
    for p in [*plan.order, 0]:
        if p != plan.order[0]:
            part = mix_back(plan, p, rounded, state_kernel)
        pieces[p] = shifted(part, "state", p) if p else part
    total = None
    for p in [0, *plan.order]:
        out = backward(
            plan, p, sources, kept[p], pieces[p], total, p == plan.order[-1]
        )
        total = out[-1]
    own_part, to_left, to_right, to_far = out[0], out[1], out[2], out[3:-1]
    from_left, from_right = send_near(to_left, to_right)
    arrived = send_far(plan, to_far)
    out = divide(plan, asked, own_part, from_right, from_left, arrived, nu, final)
    return potential_u, out


def per_device(kern_blocks, kern_cols, state_kernel, start_v, mu, nu):
    plan = Plan(kern_blocks, start_v)
    shape = (plan.rows, plan.size, plan.cols)
    nu = nu.reshape(shape)
    kept = [None] * plan.states
    for sweep in range(ITERS):
        if sweep == 0:
            sources, asks, (own, head, tail) = begin(plan, kern_cols, start_v.reshape(shape))
            asked = send_asks(plan, asks)
            state = (own, head, tail, first_far(plan, asked, own))
        potential_u, out = sweep_once(
            plan,
            state,
            sources,
            asked,
            kern_blocks,
            kept,
            state_kernel,
            mu,
            nu,
            sweep == 0,
            sweep == ITERS - 1,
        )
        state = (out[0], *out[1:3], out[3:])
    return (potential_u, out[0].reshape(start_v.shape))


def solution(mesh):
    placed = (
        P("mesh", None, None, None),
        P("mesh", None),
        P(),
        P("mesh", "state"),
        P(("mesh", "state"), None),
        P("mesh", "state"),
    )
    return jax.shard_map(
        per_device,
        mesh=mesh,
        in_specs=placed,
        out_specs=(P(("mesh", "state"), None), P("mesh", "state")),
        check_vma=False,
    )
```

```python
import jax
import jax.numpy as jnp
from jax import lax
from jax.experimental import pallas as pl
from jax.experimental.pallas import tpu as pltpu
from jax.sharding import PartitionSpec as P

CAP_FAR = 2
ITERS = 2
CAP_NEAR = 6


VMEM = pl.BlockSpec(memory_space=pltpu.VMEM)
SMEM = pl.BlockSpec(memory_space=pltpu.SMEM)
INDEX = pl.BlockSpec(memory_space=pltpu.SMEM)
ANY = pl.BlockSpec(memory_space=pl.ANY)
HBM = pl.BlockSpec(memory_space=pltpu.HBM)
PARAMS = pltpu.CompilerParams(vmem_limit_bytes=16 << 20)
F32, BF16 = jnp.float32, jnp.bfloat16
MOST_SHIFTS = 8
CHUNKS = 2


def in_smem(value):
    return pltpu.with_memory_space_constraint(value, pltpu.SMEM)


def in_hbm(value):
    return pltpu.with_memory_space_constraint(value, pltpu.HBM)


def here(value):
    return pltpu.with_memory_space_constraint(value, pltpu.VMEM)


def shifted(value, axis, steps):
    count = lax.axis_size(axis)
    return lax.ppermute(value, axis, [(i, (i + steps) % count) for i in range(count)])


def swapped(value, axis):
    return lax.all_to_all(value, axis, split_axis=0, concat_axis=0, tiled=True)


class Plan:
    def __init__(self, kern_blocks, start_v):
        self.rows, self.degree, self.size, _ = kern_blocks.shape
        self.cols = start_v.shape[1]
        self.peers = lax.axis_size("mesh")
        self.states = lax.axis_size("state")
        self.near, self.far = CAP_NEAR, CAP_FAR
        self.far_base = self.rows + 2 * self.near
        self.table = self.far_base + self.peers * self.far
        self.share = self.rows // self.states
        self.shifts = range(2, self.peers - 1) if self.peers <= MOST_SHIFTS else None
        self.chunks = CHUNKS if self.share % CHUNKS == 0 else 1
        self.group = self.share // self.chunks

    def blocks(self, count, dtype):
        return pltpu.VMEM((count, self.size, self.cols), dtype)

    def far_blocks(self):
        if self.shifts is None:
            return [self.blocks(self.peers * self.far, BF16)]
        return [self.blocks(self.far, BF16)] * len(self.shifts)

    def far_slots(self, way):
        if self.shifts is None:
            return [(t, 0, t) for t in range(self.peers * self.far)]
        slots = []
        for i, shift in enumerate(self.shifts):
            peer = lax.rem(lax.axis_index("mesh") + way * shift + self.peers, self.peers)
            slots += [(peer * self.far + t, i, t) for t in range(self.far)]
        return slots

    def cost(self, matmul_blocks, nbytes):
        flops = 2 * matmul_blocks * self.size * self.size * self.cols
        return pl.CostEstimate(flops=flops, bytes_accessed=nbytes, transcendentals=0)

    def rows_of(self, p, chunk):
        share = lax.rem(lax.axis_index("state") - p + self.states, self.states)
        return share * self.share + chunk * self.group


def call(kernel, out_shape, in_specs, args, cost, scratch=(), aliases={}, out_specs=None):
    args = [here(a) if spec is VMEM else a for spec, a in zip(in_specs, args)]
    args = [in_smem(a) if spec is INDEX else a for spec, a in zip(in_specs, args)]
    args = [in_hbm(a) if spec is HBM else a for spec, a in zip(in_specs, args)]
    return pl.pallas_call(
        kernel,
        out_shape=out_shape,
        in_specs=in_specs,
        out_specs=[VMEM] * len(out_shape) if out_specs is None else out_specs,
        scratch_shapes=list(scratch),
        input_output_aliases=aliases,
        compiler_params=PARAMS,
        cost_estimate=cost,
    )(*args)


def begin(plan, kern_cols, start_v):
    rows, near, peers, far = plan.rows, plan.near, plan.peers, plan.far
    n_ask = 1 if plan.shifts is None else len(plan.shifts)

    def kernel(cols_ref, v_hbm, src_ref, *rest):
        asks, (own, head, tail, buf, src_buf, sem) = rest[:n_ask], rest[n_ask:]
        load = pltpu.make_async_copy(v_hbm, buf, sem)
        load.start()
        me = lax.axis_index("mesh")
        cols = cols_ref[...]
        before, after = lax.rem(me + peers - 1, peers), lax.rem(me + 1, peers)
        src = cols - me * rows + near
        src = jnp.where(cols // rows == before, cols - before * rows - (rows - near), src)
        src = jnp.where(cols // rows == after, cols - after * rows + near + rows, src)
        for d in range(peers) if plan.shifts is None else plan.shifts:
            peer = d if plan.shifts is None else lax.rem(me + d, peers)
            place = cols - peer * rows
            of_peer = (place >= 0) & (place < rows)
            if plan.shifts is None:
                of_peer &= (peer != me) & (peer != before) & (peer != after)
            least = jnp.min(jnp.where(of_peer, place, rows))
            most = jnp.max(jnp.where(of_peer, place, 0))
            slot = plan.far_base + peer * far
            src = jnp.where(of_peer, slot + (place != least).astype(jnp.int32), src)
            ask, at = (asks[0], d * far) if plan.shifts is None else (asks[d - 2], 0)
            ask[at] = jnp.minimum(least, most)
            ask[at + 1] = most
        src_buf[...] = src
        load.wait()
        index = pltpu.make_async_copy(src_buf, src_ref, sem)
        index.start()
        for t in range(rows):
            value = buf[t].astype(BF16)
            own[t] = value
            if t < near:
                head[t] = value
            if t >= rows - near:
                tail[t - rows + near] = value
        index.wait()

    ask = jax.ShapeDtypeStruct((peers * far if plan.shifts is None else far,), jnp.int32)
    out = call(
        kernel,
        [pltpu.SMEM(kern_cols.shape, jnp.int32)]
        + [ask] * n_ask
        + [plan.blocks(n, BF16) for n in (rows, near, near)],
        [VMEM, HBM],
        [kern_cols, start_v],
        plan.cost(0, 3 << 20),
        [
            pltpu.VMEM(start_v.shape, F32),
            pltpu.VMEM(kern_cols.shape, jnp.int32),
            pltpu.SemaphoreType.DMA,
        ],
        out_specs=[INDEX] + [SMEM] * n_ask + [VMEM] * 3,
    )
    return out[0], list(out[1 : 1 + n_ask]), out[1 + n_ask :]


def forward(plan, chunk, sources, kern, inputs, table, first_time):
    group, degree, near, rows = plan.group, plan.degree, plan.near, plan.rows
    states = plan.states
    gathers = table is None
    n_in = len(inputs) if gathers else 1

    def kernel(src, kern_ref, *rest):
        ins, outs = rest[:n_in], rest[n_in:]
        tbl = outs[states] if gathers else ins[0]
        firsts = [plan.rows_of(p, chunk) for p in range(states)]
        held = kern_ref
        if first_time:
            held, sem = outs[-2:]
            loads = [
                pltpu.make_async_copy(
                    kern_ref.at[firsts[p] + g], held.at[p * group + g], sem.at[p * group + g]
                )
                for p in range(states)
                for g in range(group)
            ]
            for load in loads:
                load.start()
        if gathers:
            own_ref, left_ref, right_ref = ins[:3]
            far_refs = ins[3:]
            for t in range(near):
                tbl[t] = left_ref[t]
                tbl[near + rows + t] = right_ref[t]
            for t in range(rows):
                tbl[near + t] = own_ref[t]
            for slot, i, t in plan.far_slots(-1):
                tbl[plan.far_base + slot] = far_refs[i][t]
        for p in range(states):
            for g in range(group):
                at, row = p * group + g, firsts[p] + g
                if first_time:
                    loads[at].wait()
                lhs = jnp.concatenate([held[at, k] for k in range(degree)], axis=1)
                rhs = jnp.concatenate([tbl[src[row, k]] for k in range(degree)], axis=0)
                outs[p][g] = jnp.dot(lhs, rhs, preferred_element_type=F32).astype(BF16)

    out_shape = [plan.blocks(group, BF16)] * states
    if gathers:
        out_shape.append(plan.blocks(plan.table, BF16))
    if first_time:
        out_shape.append(pltpu.VMEM((states * group, *kern.shape[1:]), BF16))
    out = call(
        kernel,
        out_shape,
        [INDEX, HBM if first_time else VMEM] + [VMEM] * n_in,
        [sources, kern] + (list(inputs) if gathers else [table]),
        plan.cost(states * group * degree, 6 << 20),
        [pltpu.SemaphoreType.DMA((states * group,))] if first_time else (),
    )
    return out[:states], out[states] if gathers else table, out[-1] if first_time else kern


def turned(plan, k_ref, p):
    at = lax.rem(lax.axis_index("state") + p, plan.states) * plan.cols
    return k_ref[:, pl.ds(pl.multiple_of(at, plan.cols), plan.cols)]


def mix(plan, chunk, pieces, state_kernel, mu, u_so_far, final):
    states, group, size, cols = plan.states, plan.group, plan.size, plan.cols
    passed = final and u_so_far is not None

    def kernel(*refs):
        a_refs, (k_ref, mu_ref), rest = refs[:states], refs[states : states + 2], refs[states + 2 :]
        if passed:
            rest = rest[1:]
        outs, rest = rest[:states], rest[states:]
        k_all = jnp.concatenate([turned(plan, k_ref, p) for p in range(states)], axis=1)
        copies = []
        for g in range(group):
            a = jnp.concatenate([ref[g] for ref in a_refs], axis=1)
            mixed = lax.dot_general(a, k_all, (((1,), (1,)), ((), ())), preferred_element_type=F32)
            at = (chunk * group + g) * size
            u = mu_ref[pl.ds(at, size), :] / mixed
            if final:
                u_ref, u_buf, sem = rest
                u_buf[g] = u
                copy = pltpu.make_async_copy(u_buf.at[g], u_ref.at[pl.ds(at, size), :], sem.at[g])
                copy.start()
                copies.append(copy)
            b = jnp.dot(u.astype(BF16), k_all, preferred_element_type=F32).astype(BF16)
            for p in range(states):
                outs[p][g] = b[:, p * cols : (p + 1) * cols]
        for copy in copies:
            copy.wait()

    args, in_specs = [*pieces, state_kernel, mu], [VMEM] * (states + 2)
    out_shape = [plan.blocks(group, BF16)] * states
    out_specs, scratch, aliases = [VMEM] * states, [], {}
    if final:
        out_shape = out_shape + [jax.ShapeDtypeStruct(mu.shape, F32)]
        out_specs = out_specs + [ANY]
        scratch = [pltpu.VMEM((group, size, mu.shape[1]), F32), pltpu.SemaphoreType.DMA((group,))]
        if passed:
            aliases = {len(args): states}
            args.append(u_so_far)
            in_specs.append(ANY)
    out = call(
        kernel,
        out_shape,
        in_specs,
        args,
        plan.cost(2 * group * states * states, 3 << 20),
        scratch,
        aliases,
        out_specs,
    )
    return out[:states], out[states] if final else None


def backward(plan, chunk, sources, kern, pieces, so_far):
    group, degree, near, rows = plan.group, plan.degree, plan.near, plan.rows
    states = plan.states
    n_acc = 0 if so_far is None else 1
    last = chunk == plan.chunks - 1

    def kernel(src, kern_ref, *rest):
        b_refs, rest = rest[:states], rest[states + n_acc :]
        acc = rest[-1]
        if not n_acc:
            acc[...] = jnp.zeros_like(acc)
        for p in range(states):
            first = plan.rows_of(p, chunk)
            for g in range(group):
                b = b_refs[p][g]
                for k in range(degree):
                    part = lax.dot_general(
                        kern_ref[p * group + g, k],
                        b,
                        (((0,), (0,)), ((), ())),
                        preferred_element_type=F32,
                    )
                    acc[src[first + g, k]] += part
        if not last:
            return
        own, left, right, far = rest[0], rest[1], rest[2], rest[3:-1]
        for t in range(near):
            left[t] = acc[t].astype(BF16)
            right[t] = acc[near + rows + t].astype(BF16)
        for slot, i, t in plan.far_slots(1):
            far[i][t] = acc[plan.far_base + slot].astype(BF16)
        for t in range(rows):
            own[t] = acc[near + t].astype(BF16)

    out_shape = []
    if last:
        out_shape = [plan.blocks(n, BF16) for n in (rows, near, near)] + plan.far_blocks()
    return call(
        kernel,
        out_shape + [plan.blocks(plan.table, F32)],
        [INDEX] + [VMEM] * (1 + states + n_acc),
        [sources, kern, *pieces] + ([] if so_far is None else [so_far]),
        plan.cost(states * group * degree, 10 << 20),
        (),
        {2 + states: len(out_shape)} if n_acc else {},
    )


def first_far(plan, asked, own):
    def kernel(own_ref, *rest):
        asked_refs, outs = rest[: len(asked)], rest[len(asked) :]
        for _, i, t in plan.far_slots(1):
            outs[i][t] = own_ref[asked_refs[i][t]]

    return call(
        kernel,
        plan.far_blocks(),
        [VMEM] + [SMEM] * len(asked),
        [own, *asked],
        plan.cost(0, 2 << 20),
    )


def divide(plan, asked, own, from_right, from_left, arrived, nu, final):
    near, rows, n_far = plan.near, plan.rows, len(arrived)

    def kernel(own_ref, right_ref, left_ref, nu_ref, *rest):
        far_refs, asked_refs, outs, acc = (
            rest[:n_far],
            rest[n_far : 2 * n_far],
            rest[2 * n_far : -1],
            rest[-1],
        )
        for t in range(rows):
            value = own_ref[t].astype(F32)
            if t < near:
                value = value + left_ref[t].astype(F32)
            if t >= rows - near:
                value = value + right_ref[t - rows + near].astype(F32)
            acc[t] = value
        for _, i, t in plan.far_slots(-1):
            acc[asked_refs[n_far - 1 - i][t]] += far_refs[i][t].astype(F32)
        for t in range(rows):
            value = nu_ref[t] / acc[t]
            if final:
                outs[0][t] = value
            else:
                value = value.astype(BF16)
                outs[0][t] = value
                if t < near:
                    outs[1][t] = value
                if t >= rows - near:
                    outs[2][t - rows + near] = value
        if not final:
            for _, i, t in plan.far_slots(1):
                outs[3 + i][t] = outs[0][asked_refs[i][t]]

    if final:
        out_shape = [jax.ShapeDtypeStruct((rows, plan.size, plan.cols), F32)]
    else:
        out_shape = [plan.blocks(n, BF16) for n in (rows, near, near)] + plan.far_blocks()
    return call(
        kernel,
        out_shape,
        [VMEM] * (4 + n_far) + [SMEM] * n_far,
        [own, from_right, from_left, nu, *arrived, *asked],
        plan.cost(0, 6 << 20),
        [pltpu.VMEM((rows, plan.size, plan.cols), F32)],
    )


def send_far(plan, pieces):
    if plan.shifts is None:
        return [swapped(pieces[0], "mesh")]
    out = []
    for d, piece in zip(plan.shifts, pieces):
        out.append(shifted(piece, "mesh", d))
    return out


def send_asks(plan, asks):
    if plan.shifts is None:
        pairs = asks[0].reshape(plan.peers, plan.far)
        return [swapped(pairs, "mesh").reshape(-1)]
    return send_far(plan, asks)[::-1]


def send_near(to_left, to_right):
    from_left = shifted(to_right, "mesh", 1)
    from_right = shifted(to_left, "mesh", -1)
    return from_left, from_right


def sweep_once(plan, state, sources, asked, kern, kept, state_kernel, mu, nu, first_time, final):
    own, head, tail, far = state
    from_left, from_right = send_near(head, tail)
    far = send_far(plan, far)
    inputs, table = [own, from_left, from_right, *far], None
    spread, returned = [], []
    for c in range(plan.chunks):
        parts, table, kept[c] = forward(
            plan, c, sources, kern if first_time else kept[c], inputs, table, first_time
        )
        spread.append([parts[0]] + [shifted(parts[p], "state", -p) for p in range(1, plan.states)])
    potential_u = None
    for c in range(plan.chunks):
        parts, potential_u = mix(plan, c, spread[c], state_kernel, mu, potential_u, final)
        returned.append([parts[0]] + [shifted(parts[p], "state", p) for p in range(1, plan.states)])
    total = None
    for c in range(plan.chunks):
        out = backward(plan, c, sources, kept[c], returned[c], total)
        total = out[-1]
    own_part, to_left, to_right, to_far = out[0], out[1], out[2], out[3:-1]
    from_left, from_right = send_near(to_left, to_right)
    arrived = send_far(plan, to_far)
    out = divide(plan, asked, own_part, from_right, from_left, arrived, nu, final)
    return potential_u, out


def per_device(kern_blocks, kern_cols, state_kernel, start_v, mu, nu):
    plan = Plan(kern_blocks, start_v)
    shape = (plan.rows, plan.size, plan.cols)
    nu = nu.reshape(shape)
    kept = [None] * plan.chunks
    for sweep in range(ITERS):
        if sweep == 0:
            sources, asks, (own, head, tail) = begin(plan, kern_cols, start_v.reshape(shape))
            asked = send_asks(plan, asks)
            state = (own, head, tail, first_far(plan, asked, own))
        potential_u, out = sweep_once(
            plan,
            state,
            sources,
            asked,
            kern_blocks,
            kept,
            state_kernel,
            mu,
            nu,
            sweep == 0,
            sweep == ITERS - 1,
        )
        state = (out[0], *out[1:3], out[3:])
    return (potential_u, out[0].reshape(start_v.shape))


def solution(mesh):
    placed = (
        P("mesh", None, None, None),
        P("mesh", None),
        P(),
        P("mesh", "state"),
        P(("mesh", "state"), None),
        P("mesh", "state"),
    )
    return jax.shard_map(
        per_device,
        mesh=mesh,
        in_specs=placed,
        out_specs=(P(("mesh", "state"), None), P("mesh", "state")),
        check_vma=False,
    )
```
